32 devices in a mesh: ens: 2 (over x), lat: 4 (over y, core), lon: 4 (over z).
Axes of the slice: x: 2, y: 2, z: 4, core: 2. Of those that a mesh axis runs over, the one named last changes fastest.
Arguments:
- field_in: bfloat16 [64, 512, 256], P(('ens', 'lat'), 'lon'), parts along dimension 0, may hold values from -6 to 6
- quadrature: float32 [32, 3, 8, 129], P('lat'), may hold values from -6 to 6
- half_width: int32 [32], P('lat'), may hold values from 1 to 64, as said below
- mixing: bfloat16 [8, 256, 256], replicated, may hold values from -0.125 to 0.125
- cotangent: bfloat16 [64, 512, 256], P(('ens', 'lat'), 'lon'), parts along dimension 0, may hold values from -6 to 6
Outputs:
- field_out: bfloat16 [64, 512, 256], P(('ens', 'lat'), 'lon'), parts along dimension 0
- input_grad: bfloat16 [64, 512, 256], P(('ens', 'lat'), 'lon'), parts along dimension 0
- weight_grad: float32 [8, 512, 256], P('lon', 'ens'), parts along dimension 1
The draws below stay inside these ranges and needn't reach their ends.
There are 2 independent parts, one for each index of `ens`. The reference program is written for one: setup_inputs(seed, part) draws one part's arguments, and reference() takes and returns one part's arrays. A program takes and returns all parts, laid end to end along the dimension named above; an argument that names none is the same for every part. Nothing has to cross between parts.
Inputs may be any that keep to these rules, and one draw needn't show every extreme that they name: `half_width`: 64 is reached at the polar rows in every draw.
All inputs are finite; a program needn't handle non-finite values.
Results may differ from the reference program's by a relative error of at most 0.0058.
Values may be sent and summed in bfloat16 or wider, within the bound.
No kernel may reach another device: no remote copies, remote signals or barrier semaphores. Data moves between devices by JAX's collectives and lax.ppermute only.
A program may use at most 128 MiB of HBM per device.

```python
import jax
import jax.numpy as jnp
from jax import lax

C = 256
K = 8
HW = 64
TAPS = 129
NLAT = 32
NLON = 512


def draw_half_width(key, part):
    row_ids = jnp.arange(NLAT, dtype=jnp.int32)
    to_pole = jnp.minimum(row_ids, NLAT - 1 - row_ids)
    jitter = jax.random.randint(key, (NLAT,), 0, 3, dtype=jnp.int32)
    return jnp.clip(2 * HW // (to_pole + 2) + jitter, 1, HW).astype(jnp.int32)


def block_scale(key, extent, shards, smallest, largest):
    def one(dim, blocks):
        heights = jax.random.uniform(jax.random.fold_in(jax.random.fold_in(key, 6), dim), (blocks,), jnp.float32, smallest / len(shards), largest / len(shards))
        return jnp.repeat(jnp.exp(heights), extent[dim] // blocks).reshape((-1,) + (1,) * (len(extent) - dim - 1))

    level = one(*shards[0])
    for cut in shards[1:]:
        level = level * one(*cut)
    return level


def centred(rng, shape, deviation, most, split=(), held_as=jnp.bfloat16):
    values = deviation * jax.random.normal(rng, shape, jnp.float32)
    if split:
        values = values * block_scale(rng, shape, split, -0.22, 0.18)
    return jnp.clip(values, -most, most).astype(held_as)


def setup_inputs(seed: int = 0, part: int = 0) -> dict:
    key_of = jax.random.split(jax.random.key(seed), 6)
    part_keys = jax.random.split(jax.random.fold_in(key_of[5], part), 6)
    field_in = centred(part_keys[0], (NLAT, NLON, C), 1.0, 6.0, ((0, 4), (1, 4)))
    quadrature = centred(key_of[1], (NLAT, 3, K, TAPS), 1.0, 6.0, ((0, 4),), jnp.float32)
    half_width = draw_half_width(jax.random.fold_in(key_of[5], 71), part)
    mixing = centred(key_of[3], (K, C, C), (K * C) ** -0.5, 0.125)
    cotangent = centred(part_keys[4], (NLAT, NLON, C), 1.0, 6.0, ((0, 4), (1, 4)))
    return {"field_in": field_in, "quadrature": quadrature, "half_width": half_width, "mixing": mixing, "cotangent": cotangent}


def scaled_basis(quadrature, half_width):
    offsets = jnp.abs(jnp.arange(TAPS, dtype=jnp.int32) - HW)
    counts = 3.0 * (2.0 * half_width.astype(jnp.float32) + 1.0)
    factor = 1.0 / jnp.sqrt(counts)
    inside = (offsets[None, :] <= half_width[:, None]).astype(jnp.float32)
    return (quadrature * factor[:, None, None, None] * inside[:, None, None, :]).astype(jnp.bfloat16)

def periodic(field):
    return jnp.concatenate([field[:, NLON - HW:], field, field[:, :HW]], axis=1)

def correlate(lhs_array, rhs_array):
    return lax.conv_general_dilated(lhs_array, rhs_array, (1,), 'VALID', dimension_numbers=('NCH', 'OIH', 'NCH'), precision=lax.Precision.HIGHEST)

def reference(field_in, quadrature, half_width, mixing, cotangent):
    basis = scaled_basis(quadrature, half_width)
    padded = jnp.pad(periodic(field_in), ((1, 1), (0, 0), (0, 0)))

    def forward_row(row_index):
        row_block = lax.dynamic_slice_in_dim(padded, row_index, 3, 0).astype(jnp.float32)
        lhs_array = jnp.transpose(row_block, (2, 0, 1))
        rhs_array = jnp.transpose(basis[row_index].astype(jnp.float32), (1, 0, 2))
        result = correlate(lhs_array, rhs_array)
        return jnp.transpose(result, (2, 1, 0)).astype(jnp.bfloat16)
    row_ids = jnp.arange(NLAT, dtype=jnp.int32)
    filtered = lax.map(forward_row, row_ids)
    flat_filtered = filtered.reshape(NLAT * NLON, K * C)
    flat_mixing = mixing.reshape(K * C, C)
    field_out = jnp.dot(flat_filtered, flat_mixing, preferred_element_type=jnp.float32).astype(jnp.bfloat16).reshape(NLAT, NLON, C)
    flat_grad = cotangent.reshape(NLAT * NLON, C)
    weight_grad = jnp.dot(flat_filtered.T, flat_grad, preferred_element_type=jnp.float32).reshape(K, C, C)
    mixed_grad = jnp.dot(flat_grad, flat_mixing.T, preferred_element_type=jnp.float32).astype(jnp.bfloat16).reshape(NLAT, NLON, K, C)
    mixed_pad = periodic(mixed_grad)
    flipped = basis[..., ::-1]

    def backward_row(row_index):
        lhs_array = jnp.transpose(mixed_pad[row_index].astype(jnp.float32), (2, 1, 0))
        rhs_array = flipped[row_index].astype(jnp.float32)
        result = correlate(lhs_array, rhs_array)
        return jnp.transpose(result, (1, 2, 0))
    contrib = lax.map(backward_row, row_ids)
    zero_row = jnp.zeros((1, NLON, C), jnp.float32)
    from_next = jnp.concatenate([contrib[1:, 0], zero_row], axis=0)
    from_prev = jnp.concatenate([zero_row, contrib[:-1, 2]], axis=0)
    input_grad = (from_next + contrib[:, 1] + from_prev).astype(jnp.bfloat16)
    return (field_out, input_grad, weight_grad)
```

```python
import functools

import jax
import jax.numpy as jnp
from jax import lax
from jax.experimental import pallas as pl
from jax.experimental.pallas import tpu as pltpu
from jax.sharding import PartitionSpec as P


BLOCK = 32
DEPTH = 256


def ring(axis, distance):
    count = lax.axis_size(axis)
    return [(i, (i + distance) % count) for i in range(count)]


def line(axis, distance):
    count = lax.axis_size(axis)
    return [(i, i + distance) for i in range(count) if 0 <= i + distance < count]


def swap(axis, mask):
    return [(i, i ^ mask) for i in range(lax.axis_size(axis))]


def scaled_basis(quadrature, half_width):
    tap_count = quadrature.shape[-1]
    offsets = jnp.abs(jnp.arange(tap_count, dtype=jnp.int32) - (tap_count - 1) // 2)
    counts = 3.0 * (2.0 * half_width.astype(jnp.float32) + 1.0)
    factor = 1.0 / jnp.sqrt(counts)
    inside = (offsets[None, :] <= half_width[:, None]).astype(jnp.float32)
    return (quadrature * factor[:, None, None, None] * inside[:, None, None, :]).astype(
        jnp.bfloat16
    )


def packed_taps(basis):
    rows, three, kernels, taps = basis.shape
    window = taps - 1 + BLOCK
    padded = jnp.pad(basis, ((0, 0), (0, 0), (0, 0), (0, window - taps)))
    flat = jnp.transpose(padded, (0, 2, 1, 3)).reshape(rows, kernels, three * window)
    total = -(-three * window // DEPTH) * DEPTH
    return jnp.pad(flat, ((0, 0), (0, 0), (0, total - three * window))).astype(jnp.float32)


def fill_extended(ext, left, own, right, top, bottom):
    rows, cols = own.shape[0], own.shape[1]
    rim = left.shape[1]
    ext[0:1] = top[...]
    ext[rows + 1 : rows + 2] = bottom[...]
    ext[1 : rows + 1, 0:rim, :] = left[...]
    ext[1 : rows + 1, rim : rim + cols, :] = own[...]
    ext[1 : rows + 1, rim + cols :, :] = right[...]


def filter_row(row, taps, ext, band, store):
    kernels, total = taps.shape[1], taps.shape[2]
    window = ext.shape[1]
    cols = store.cols
    reach = window - cols + BLOCK
    for k in range(kernels):
        spread = jnp.broadcast_to(taps[0, k : k + 1, :], (BLOCK, total))
        rolled = pltpu.roll(spread, 0, 1, stride=1, stride_axis=0)
        band[k * BLOCK : (k + 1) * BLOCK, :] = rolled.astype(band.dtype)
    for g in range(cols // BLOCK):
        first = g * BLOCK
        pieces = [ext[row + r, first : first + reach, :] for r in range(3)]
        spare = total - 3 * reach
        if spare:
            pieces.append(ext[row, 0:spare, :])
        source = jnp.concatenate(pieces, axis=0)
        result = jnp.dot(band[...], source, preferred_element_type=jnp.float32)
        result = result.astype(jnp.bfloat16)
        for k in range(kernels):
            store(g, k, result[k * BLOCK : (k + 1) * BLOCK])


class Store:
    def __init__(self, cols, write):
        self.cols = cols
        self.write = write

    def __call__(self, g, k, value):
        self.write(g, k, value)


def forward_kernel(
    n_lat, ids, taps, left, own, right, top, bottom, cot, filt_out, keep, send, ext, band, filt, grad
):
    row = pl.program_id(0)
    cols = own.shape[1]
    chans = own.shape[2]
    kernels = taps.shape[1]

    @pl.when(row == 0)
    def _():
        fill_extended(ext, left, own, right, top, bottom)

    def write(g, k, value):
        lanes = slice(k * chans, (k + 1) * chans)
        filt_out[g * BLOCK : (g + 1) * BLOCK, lanes] = value
        start = pl.multiple_of(row * cols + g * BLOCK, BLOCK)
        filt[pl.ds(start, BLOCK), lanes] = value

    filter_row(row, taps, ext, band, Store(cols, write))

    @pl.when(row == pl.num_programs(0) - 1)
    def _():
        for k in range(kernels):
            grad[k] = lax.dot_general(
                filt[:, k * chans : (k + 1) * chans],
                cot[...],
                (((0,), (0,)), ((), ())),
                preferred_element_type=jnp.float32,
            )
        lat, lon = ids[0], ids[1]
        n_lon, share, piece = keep.shape[1], keep.shape[2], keep.shape[3]
        bits = n_lat.bit_length() - 1
        for m in range(n_lat):
            slot = sum(((m >> b) & 1) << (bits - 1 - b) for b in range(bits))
            rank = lat ^ slot
            start = pl.multiple_of(rank * piece, piece)
            for s in range(n_lon):
                first = lax.rem(lon + s, n_lon) * share
                value = grad[pl.ds(first, share), pl.ds(start, piece), :]
                if m < n_lat // 2:
                    keep[m, s] = value
                else:
                    send[m - n_lat // 2, s] = value.astype(send.dtype)


def backward_kernel(taps, left, own, right, top, bottom, mixing, out, ext, band, filt):
    row = pl.program_id(0)
    cols = own.shape[1]
    chans = own.shape[2]
    kernels = taps.shape[1]

    @pl.when(row == 0)
    def _():
        fill_extended(ext, left, own, right, top, bottom)

    def write(g, k, value):
        start = pl.multiple_of(row * cols + g * BLOCK, BLOCK)
        filt[k, pl.ds(start, BLOCK), :] = value

    filter_row(row, taps, ext, band, Store(cols, write))

    @pl.when(row == pl.num_programs(0) - 1)
    def _():
        total = None
        for k in range(kernels):
            term = lax.dot_general(
                filt[k], mixing[k], (((1,), (1,)), ((), ())), preferred_element_type=jnp.float32
            )
            total = term if total is None else total + term
        out[...] = total.astype(out.dtype)


def whole(shape):
    return pl.BlockSpec(shape, lambda i: (0,) * len(shape))


def halo_specs(taps, rim, rows, cols, chans):
    return [
        pl.BlockSpec((1,) + taps.shape[1:], lambda i: (i, 0, 0)),
        whole((rows, rim, chans)),
        whole((rows, cols, chans)),
        whole((rows, rim, chans)),
        whole((1, cols + 2 * rim, chans)),
        whole((1, cols + 2 * rim, chans)),
    ]


def forward(ids, taps, left, own, right, top, bottom, cot, n_lat, n_lon):
    rows, cols, chans = own.shape
    kernels = taps.shape[1]
    rim = left.shape[1]
    parts = (n_lat // 2, n_lon, kernels // n_lon, chans // n_lat, chans)
    return pl.pallas_call(
        functools.partial(forward_kernel, n_lat),
        grid=(rows,),
        in_specs=[pl.BlockSpec(memory_space=pltpu.SMEM)]
        + halo_specs(taps, rim, rows, cols, chans)
        + [whole((rows * cols, chans))],
        out_specs=[
            pl.BlockSpec((cols, kernels * chans), lambda i: (i, 0)),
            whole(parts),
            whole(parts),
        ],
        out_shape=[
            jax.ShapeDtypeStruct((rows * cols, kernels * chans), jnp.bfloat16),
            jax.ShapeDtypeStruct(parts, jnp.float32),
            jax.ShapeDtypeStruct(parts, jnp.bfloat16),
        ],
        scratch_shapes=[
            pltpu.VMEM((rows + 2, cols + 2 * rim, chans), jnp.bfloat16),
            pltpu.VMEM((kernels * BLOCK, taps.shape[2]), jnp.bfloat16),
            pltpu.VMEM((rows * cols, kernels * chans), jnp.bfloat16),
            pltpu.VMEM((kernels, chans, chans), jnp.float32),
        ],
        name="forward_filter",
    )(ids, taps, left, own, right, top, bottom, cot)


def backward(taps, left, own, right, top, bottom, mixing):
    rows, cols, chans = own.shape
    kernels = taps.shape[1]
    rim = left.shape[1]
    return pl.pallas_call(
        backward_kernel,
        grid=(rows,),
        in_specs=halo_specs(taps, rim, rows, cols, chans) + [whole(mixing.shape)],
        out_specs=whole((rows * cols, chans)),
        out_shape=jax.ShapeDtypeStruct((rows * cols, chans), jnp.bfloat16),
        scratch_shapes=[
            pltpu.VMEM((rows + 2, cols + 2 * rim, chans), jnp.bfloat16),
            pltpu.VMEM((kernels * BLOCK, taps.shape[2]), jnp.bfloat16),
            pltpu.VMEM((kernels, rows * cols, chans), jnp.bfloat16),
        ],
        name="backward_filter",
    )(taps, left, own, right, top, bottom, mixing)


def assemble_kernel(ids, pieces, out):
    count, share, piece, chans = pieces.shape
    bits = count.bit_length() - 1
    for p in range(count):
        slot = ids[0] ^ p
        index = sum(((slot >> b) & 1) << (bits - 1 - b) for b in range(bits))
        out[:, p * piece : (p + 1) * piece, :] = pieces[index]


def assemble(ids, pieces):
    count, share, piece, chans = pieces.shape
    return pl.pallas_call(
        assemble_kernel,
        in_specs=[
            pl.BlockSpec(memory_space=pltpu.SMEM),
            pl.BlockSpec(memory_space=pltpu.VMEM),
        ],
        out_specs=pl.BlockSpec(memory_space=pltpu.VMEM),
        out_shape=jax.ShapeDtypeStruct((share, count * piece, chans), pieces.dtype),
        name="assemble",
    )(ids, pieces)


def reduced_gradient(ids, keep, send):
    n_lat, n_lon = lax.axis_size("lat"), lax.axis_size("lon")
    mask = 1
    while True:
        total = keep + lax.ppermute(send, "lat", swap("lat", mask)).astype(jnp.float32)
        mask *= 2
        if mask >= n_lat:
            break
        half = total.shape[0] // 2
        keep, send = total[:half], total[half:].astype(jnp.bfloat16)
    total = total[0]
    wire = total.astype(jnp.bfloat16)
    piece = total[0]
    for s in range(1, n_lon):
        piece = piece + lax.ppermute(wire[s], "lon", ring("lon", s)).astype(jnp.float32)
    pieces = piece[None]
    while mask > 1:
        mask //= 2
        other = lax.ppermute(pieces, "lat", swap("lat", mask))
        pieces = jnp.concatenate([pieces, other], axis=0)
    return assemble(ids, pieces)


def on_device(field_in, quadrature, half_width, mixing, cotangent):
    rows, cols, chans = field_in.shape
    kernels, _, outs = mixing.shape
    taps = quadrature.shape[-1]
    rim = (taps - 1) // 2
    n_lat, n_lon = lax.axis_size("lat"), lax.axis_size("lon")
    ids = jnp.stack([lax.axis_index("lat"), lax.axis_index("lon")]).astype(jnp.int32)

    def beside(array):
        left = lax.ppermute(array[:, cols - rim :], "lon", ring("lon", 1))
        right = lax.ppermute(array[:, :rim], "lon", ring("lon", -1))
        return left, right

    def wide(array, left, right, row):
        return jnp.concatenate([left[row], array[row], right[row]], axis=0)

    f_left, f_right = beside(field_in)
    g_left, g_right = beside(cotangent)
    f_top = lax.ppermute(wide(field_in, f_left, f_right, rows - 1)[None], "lat", line("lat", 1))
    f_bottom = lax.ppermute(wide(field_in, f_left, f_right, 0)[None], "lat", line("lat", -1))

    basis = scaled_basis(quadrature, half_width)
    filtered, keep, send = forward(
        ids,
        packed_taps(basis),
        f_left,
        field_in,
        f_right,
        f_top,
        f_bottom,
        cotangent.reshape(rows * cols, outs),
        n_lat,
        n_lon,
    )
    weight_grad = reduced_gradient(ids, keep, send)

    def edge(row, r):
        extra = jnp.pad(basis[row, r], ((0, 0), (0, chans - taps)))
        return jnp.concatenate([wide(cotangent, g_left, g_right, row), extra], axis=0)

    span = cols + 2 * rim
    above = lax.ppermute(edge(rows - 1, 2), "lat", line("lat", 1))
    below = lax.ppermute(edge(0, 0), "lat", line("lat", -1))
    g_top, before = above[None, :span], above[span:, :taps]
    g_bottom, after = below[None, :span], below[span:, :taps]
    from_above = jnp.concatenate([before[None], basis[: rows - 1, 2]], axis=0)
    from_below = jnp.concatenate([basis[1:, 0], after[None]], axis=0)
    adjoint = jnp.stack([from_above, basis[:, 1], from_below], axis=1)[..., ::-1]
    input_grad = backward(
        packed_taps(adjoint), g_left, cotangent, g_right, g_top, g_bottom, mixing
    )
    field_out = jnp.dot(
        filtered,
        mixing.reshape(kernels * chans, outs),
        preferred_element_type=jnp.float32,
    ).astype(jnp.bfloat16)
    return (
        field_out.reshape(rows, cols, outs),
        input_grad.reshape(rows, cols, chans),
        weight_grad,
    )


def solution(mesh):
    return jax.shard_map(
        on_device,
        mesh=mesh,
        in_specs=(
            P(("ens", "lat"), "lon", None),
            P("lat", None, None, None),
            P("lat"),
            P(),
            P(("ens", "lat"), "lon", None),
        ),
        out_specs=(
            P(("ens", "lat"), "lon", None),
            P(("ens", "lat"), "lon", None),
            P("lon", "ens", None),
        ),
        check_vma=False,
    )
```

```python
import functools

import jax
import jax.numpy as jnp
from jax import lax
from jax.experimental import pallas as pl
from jax.experimental.pallas import tpu as pltpu
from jax.sharding import PartitionSpec as P


BLOCK = 32
LANES = 128
DEPTH = 256


def ring(axis, distance):
    count = lax.axis_size(axis)
    return [(i, (i + distance) % count) for i in range(count)]


def line(axis, distance):
    count = lax.axis_size(axis)
    return [(i, i + distance) for i in range(count) if 0 <= i + distance < count]


def swap(axis, mask):
    return [(i, i ^ mask) for i in range(lax.axis_size(axis))]


IN_VMEM = pl.BlockSpec(memory_space=pltpu.VMEM)
IN_SMEM = pl.BlockSpec(memory_space=pltpu.SMEM)
IN_HBM = pl.BlockSpec(memory_space=pltpu.HBM)


def near(array):
    return pltpu.with_memory_space_constraint(array, pltpu.VMEM)


def kernel_call(body, operands, outs, scratch, mib, scalars=0, far=(), far_out=False, alias=None):
    specs = [IN_SMEM] * scalars
    given = list(operands[:scalars])
    for i, operand in enumerate(operands[scalars:], scalars):
        specs.append(IN_HBM if i in far else IN_VMEM)
        given.append(operand if i in far else near(operand))
    single = not isinstance(outs, list)
    place = IN_HBM if far_out else IN_VMEM
    return pl.pallas_call(
        body,
        in_specs=specs,
        out_specs=place if single else [place] * len(outs),
        out_shape=outs,
        scratch_shapes=scratch,
        input_output_aliases=alias or {},
        compiler_params=pltpu.CompilerParams(vmem_limit_bytes=mib << 20),
    )(*given)


def packed_taps(pieces, window, total):
    kernels = pieces[0].shape[0]
    packed = None
    for r, piece in enumerate(pieces):
        wide = jnp.concatenate([piece, jnp.zeros((kernels, total - piece.shape[1]), piece.dtype)], 1)
        wide = pltpu.roll(wide, r * window, 1) if r else wide
        packed = wide if packed is None else packed + wide
    return packed


def spread_bands(packed, bands, row):
    kernels, total = packed.shape
    for k in range(kernels):
        rows = jnp.broadcast_to(packed[k : k + 1, :], (BLOCK, total))
        rolled = pltpu.roll(rows, 0, 1, stride=1, stride_axis=0)
        bands[row, k * BLOCK : (k + 1) * BLOCK, :] = rolled.astype(bands.dtype)


def bands_kernel(half_width, quadrature, bands, edges):
    rows, three, kernels, taps = quadrature.shape
    window = taps - 1 + BLOCK
    middle = (taps - 1) // 2
    lane = lax.broadcasted_iota(jnp.int32, (kernels, LANES), 1)
    for row in range(rows):
        reach = jnp.full((kernels, LANES), half_width[row], jnp.int32)
        factor = 1.0 / jnp.sqrt(3.0 * (2.0 * reach.astype(jnp.float32) + 1.0))
        head_inside = (jnp.abs(lane - middle) <= reach).astype(jnp.float32)
        tail_inside = ((lane < taps - LANES) & (lane + LANES - middle <= reach)).astype(
            jnp.float32
        )
        pieces = []
        for r in range(three):
            head = quadrature[row, r, :, 0:LANES] * factor * head_inside
            last = jnp.broadcast_to(quadrature[row, r, :, LANES:taps], (kernels, LANES))
            tail = last * factor * tail_inside
            piece = jnp.concatenate([head, tail], axis=1).astype(jnp.bfloat16)
            if row == rows - 1 and r == three - 1:
                edges[0] = piece
            if row == 0 and r == 0:
                edges[1] = piece
            pieces.append(piece.astype(jnp.float32))
        spread_bands(packed_taps(pieces, window, bands.shape[2]), bands, row)


def band_matrices(half_width, quadrature):
    rows, three, kernels, taps = quadrature.shape
    total = -(-three * (taps - 1 + BLOCK) // DEPTH) * DEPTH
    return kernel_call(
        bands_kernel,
        [half_width, quadrature],
        [
            pltpu.VMEM((rows, kernels * BLOCK, total), jnp.bfloat16),
            pltpu.VMEM((2, kernels, 2 * LANES), jnp.bfloat16),
        ],
        [],
        8,
        scalars=1,
    )


def split_rows(rows):
    part = max(1, rows // 4)
    outer = list(range(part)) + list(range(rows - part, rows))
    return outer, list(range(part, rows - part))


def rims_kernel(groups, array, *refs):
    *outs, edges, sems = refs
    rows, cols = array.shape[0], array.shape[1]
    rim = outs[0].shape[1]
    copies = []
    for g, group in enumerate(groups):
        place = 0
        while place < len(group):
            size = 1
            while place + size < len(group) and group[place + size] == group[place] + size:
                size += 1
            source = array.at[pl.ds(group[place], size)]
            for side, first in ((0, cols - rim), (1, 0)):
                copies.append(
                    (
                        source.at[:, pl.ds(first, rim), :],
                        outs[2 * g + side].at[pl.ds(place, size)],
                    )
                )
            place += size
    copies.append((array.at[0], edges.at[0]))
    copies.append((array.at[rows - 1], edges.at[1]))
    copies = [pltpu.make_async_copy(*c, sems.at[i]) for i, c in enumerate(copies)]
    for copy in copies:
        copy.start()
    for copy in copies:
        copy.wait()


def rims(array, rim, groups):
    _, cols, chans = array.shape
    outs = [
        pltpu.VMEM((len(group), rim, chans), jnp.bfloat16) for group in groups for _ in range(2)
    ]
    outs.append(pltpu.VMEM((2, cols, chans), jnp.bfloat16))
    return kernel_call(
        functools.partial(rims_kernel, groups),
        [array],
        outs,
        [pltpu.SemaphoreType.DMA((16,))],
        4,
        far=(0,),
    )


def edges_kernel(picks, own, left, right, *rest):
    *basis, bottom_row, top_row = rest
    rim, cols = left.shape[1], own.shape[1]
    for i, out in ((1, bottom_row), (0, top_row)):
        out[0:rim] = left[picks[i]]
        out[rim : rim + cols] = own[i]
        out[rim + cols : 2 * rim + cols] = right[picks[i]]
        if basis:
            out[2 * rim + cols :] = basis[0][1 - i]


def edge_rows(own, left, right, picks, basis):
    _, cols, chans = own.shape
    span = cols + 2 * left.shape[1] + (basis[0].shape[1] if basis else 0)
    outs = [pltpu.VMEM((span, chans), jnp.bfloat16)] * 2
    return kernel_call(
        functools.partial(edges_kernel, picks), [own, left, right, *basis], outs, [], 4
    )


def fill_extended(ext, own, top, bottom, groups, sides):
    rows, cols = own.shape[0], own.shape[1]
    rim = sides[0].shape[1]
    span = ext.shape[1]
    ext[0] = top[0:span]
    ext[rows + 1] = bottom[0:span]
    ext[1 : rows + 1, rim : rim + cols, :] = own[...]
    for g, group in enumerate(groups):
        for i, row in enumerate(group):
            ext[row + 1, 0:rim, :] = sides[2 * g][i]
            ext[row + 1, rim + cols :, :] = sides[2 * g + 1][i]


def filter_rows(bands, ext, cols, write):
    rows, height, total = bands.shape
    reach = ext.shape[1] - cols + BLOCK
    spare = total - 3 * reach

    def one(row, carry):
        for g in range(cols // BLOCK):
            first = g * BLOCK
            pieces = [ext[row + r, first : first + reach, :] for r in range(3)]
            if spare:
                pieces.append(ext[row, 0:spare, :])
            source = jnp.concatenate(pieces, axis=0)
            result = jnp.dot(bands[row], source, preferred_element_type=jnp.float32)
            result = result.astype(jnp.bfloat16)
            start = pl.multiple_of(row * cols + first, BLOCK)
            for k in range(height // BLOCK):
                write(start, k, result[k * BLOCK : (k + 1) * BLOCK])
        return carry

    lax.fori_loop(0, rows, one, 0)


def forward_kernel(n_lat, groups, ids, bands, own, top, bottom, cot, *rest):
    *sides, filt, keep, send, ext, grad = rest
    _, cols, chans = own.shape
    kernels = grad.shape[0]
    fill_extended(ext, own, top, bottom, groups, sides)

    def write(start, k, value):
        filt[pl.ds(start, BLOCK), k * chans : (k + 1) * chans] = value

    filter_rows(bands, ext, cols, write)
    for k in range(kernels):
        grad[k] = lax.dot_general(
            filt[:, k * chans : (k + 1) * chans],
            cot[...],
            (((0,), (0,)), ((), ())),
            preferred_element_type=jnp.float32,
        )
    lat, lon = ids[0], ids[1]
    n_lon, share, piece = keep.shape[1], keep.shape[2], keep.shape[3]
    bits = n_lat.bit_length() - 1
    for m in range(n_lat):
        slot = sum(((m >> b) & 1) << (bits - 1 - b) for b in range(bits))
        start = pl.multiple_of((lat ^ slot) * piece, piece)
        for s in range(n_lon):
            first = lax.rem(lon + s, n_lon) * share
            value = grad[pl.ds(first, share), pl.ds(start, piece), :]
            if m < n_lat // 2:
                keep[m, s] = value
            else:
                send[m - n_lat // 2, s] = value.astype(send.dtype)


def forward(ids, bands, own, top, bottom, cot, groups, sides, kernels, n_lat, n_lon):
    rows, cols, chans = own.shape
    rim = sides[0].shape[1]
    parts = (n_lat // 2, n_lon, kernels // n_lon, chans // n_lat, chans)
    return kernel_call(
        functools.partial(forward_kernel, n_lat, groups),
        [ids, bands, own, top, bottom, cot, *sides],
        [
            pltpu.VMEM((rows * cols, kernels * chans), jnp.bfloat16),
            pltpu.VMEM(parts, jnp.float32),
            pltpu.VMEM(parts, jnp.bfloat16),
        ],
        [
            pltpu.VMEM((rows + 2, cols + 2 * rim, chans), jnp.bfloat16),
            pltpu.VMEM((kernels, chans, chans), jnp.float32),
        ],
        20,
        scalars=1,
    )


def mix_kernel(filt, mixing, out):
    out[...] = jnp.dot(filt[...], mixing[...], preferred_element_type=jnp.float32).astype(out.dtype)


def mirror(size):
    across = lax.broadcasted_iota(jnp.int32, (size, size), 0)
    down = lax.broadcasted_iota(jnp.int32, (size, size), 1)
    return (across + down == size - 1).astype(jnp.float32).astype(jnp.bfloat16)


def adjoint_band(window, above, here, below):
    total = here.shape[1]
    sources = [below, here, above]
    lane = lax.broadcasted_iota(jnp.int32, (here.shape[0], LANES), 1)
    tiles = []
    for first in range(0, total, LANES):
        r = min(first // window, 2)
        tile = sources[r][:, first : first + LANES]
        cut = (r + 1) * window - first
        if r < 2 and cut < LANES:
            following = sources[r + 1][:, first : first + LANES]
            tile = jnp.where(lane < cut, tile, following)
        tiles.append(tile)
    return jnp.concatenate(tiles, axis=1)


def adjoint_row(band, reversed_rows, cols, write):
    span = reversed_rows[0].shape[0]
    reach = span - cols + BLOCK
    spare = band.shape[1] - 3 * reach
    for g in range(cols // BLOCK):
        first = g * BLOCK
        pieces = [source[first : first + reach, :] for source in reversed_rows]
        if spare:
            pieces.append(reversed_rows[0][0:spare, :])
        result = jnp.dot(
            band, jnp.concatenate(pieces, axis=0), preferred_element_type=jnp.float32
        ).astype(jnp.bfloat16)
        for k in range(result.shape[0] // BLOCK):
            write(first, k, result[k * BLOCK : (k + 1) * BLOCK])


def mixed_back(filt, mixing, stage, cols):
    kernels = mixing.shape[0]
    total = None
    for k in range(kernels):
        term = lax.dot_general(
            filt[k], mixing[k], (((1,), (1,)), ((), ())), preferred_element_type=jnp.float32
        )
        total = term if total is None else total + term
    total = total.astype(jnp.bfloat16)
    flip = mirror(cols)
    for i in range(stage.shape[0]):
        row = jnp.dot(flip, total[i * cols : (i + 1) * cols], preferred_element_type=jnp.float32)
        stage[i] = row.astype(stage.dtype)


def backward_inner_kernel(window, bands, own, mixing, left, right, out, reverse, filt, stage, sem):
    rows, cols, _ = own.shape
    flip = mirror(reverse.shape[1])

    def turn(row, carry):
        line = jnp.concatenate([left[row], own[row], right[row]], axis=0)
        reverse[row] = jnp.dot(flip, line, preferred_element_type=jnp.float32).astype(
            reverse.dtype
        )
        return carry

    lax.fori_loop(0, rows, turn, 0)

    def one(step, carry):
        row = step + 1
        band = adjoint_band(window, bands[row - 1], bands[row], bands[row + 1])
        base = step * cols

        def write(first, k, value):
            filt[k, pl.ds(pl.multiple_of(base + first, BLOCK), BLOCK), :] = value

        lines = [reverse.at[row + 1], reverse.at[row], reverse.at[row - 1]]
        adjoint_row(band, lines, cols, write)
        return carry

    lax.fori_loop(0, rows - 2, one, 0)
    mixed_back(filt, mixing, stage, cols)
    copy = pltpu.make_async_copy(stage, out.at[pl.ds(1, rows - 2)], sem)
    copy.start()
    copy.wait()


def backward_inner(bands, own, mixing, left, right, window):
    rows, cols, outs = own.shape
    span = cols + 2 * left.shape[1]
    kernels, chans, _ = mixing.shape
    return kernel_call(
        functools.partial(backward_inner_kernel, window),
        [bands, own, mixing, left, right],
        jax.ShapeDtypeStruct((rows, cols, chans), jnp.bfloat16),
        [
            pltpu.VMEM((rows, span, outs), jnp.bfloat16),
            pltpu.VMEM((kernels, (rows - 2) * cols, outs), jnp.bfloat16),
            pltpu.VMEM((rows - 2, cols, chans), jnp.bfloat16),
            pltpu.SemaphoreType.DMA(()),
        ],
        16,
        far_out=True,
    )


def backward_edges_kernel(
    window, bands, top, bottom, mixing, left, right, edges, given, out,
    reverse, extra, filt, stage, sems
):
    rows = bands.shape[0]
    cols = stage.shape[1]
    span = reverse.shape[1]
    flip = mirror(span)
    lines = [top[0:span]]
    for i, row in enumerate((0, 1, rows - 2, rows - 1)):
        lines.append(jnp.concatenate([left[row], edges[i], right[row]], axis=0))
    lines.append(bottom[0:span])
    for i, line in enumerate(lines):
        reverse[i] = jnp.dot(flip, line, preferred_element_type=jnp.float32).astype(reverse.dtype)
    none = jnp.zeros((top.shape[0] - span, 2 * LANES), jnp.float32)
    above = top[span:, :].astype(jnp.float32)
    below = bottom[span:, :].astype(jnp.float32)
    spread_bands(packed_taps([none, none, above], window, bands.shape[2]), extra, 0)
    spread_bands(packed_taps([below, none, none], window, bands.shape[2]), extra, 1)
    picks = (
        (extra[0], bands[0], bands[1], 1),
        (bands[rows - 2], bands[rows - 1], extra[1], 4),
    )
    for i, (one, two, three, at) in enumerate(picks):
        band = adjoint_band(window, one, two, three)

        def write(first, k, value, base=i * cols):
            filt[k, base + first : base + first + BLOCK, :] = value

        adjoint_row(band, [reverse.at[at + 1], reverse.at[at], reverse.at[at - 1]], cols, write)
    mixed_back(filt, mixing, stage, cols)
    copies = [
        pltpu.make_async_copy(stage.at[i], out.at[row], sems.at[i])
        for i, row in enumerate((0, rows - 1))
    ]
    for copy in copies:
        copy.start()
    for copy in copies:
        copy.wait()


def backward_edges(bands, top, bottom, mixing, left, right, edges, given, window):
    _, cols, chans = given.shape
    span = cols + 2 * left.shape[1]
    kernels, _, outs = mixing.shape
    return kernel_call(
        functools.partial(backward_edges_kernel, window),
        [bands, top, bottom, mixing, left, right, edges, given],
        jax.ShapeDtypeStruct(given.shape, given.dtype),
        [
            pltpu.VMEM((6, span, outs), jnp.bfloat16),
            pltpu.VMEM((2,) + bands.shape[1:], jnp.bfloat16),
            pltpu.VMEM((kernels, 2 * cols, outs), jnp.bfloat16),
            pltpu.VMEM((2, cols, chans), jnp.bfloat16),
            pltpu.SemaphoreType.DMA((2,)),
        ],
        16,
        far=(7,),
        far_out=True,
        alias={7: 0},
    )


def assemble_kernel(ids, mine, other, out):
    half, _, piece, _ = mine.shape
    count = 2 * half
    bits = count.bit_length() - 1
    for slot in range(count):
        m = sum(((slot >> b) & 1) << (bits - 1 - b) for b in range(bits))
        source = mine[m] if m < half else other[m - half]
        start = pl.multiple_of((ids[0] ^ slot) * piece, piece)
        out[:, pl.ds(start, piece), :] = source.astype(out.dtype)


def assemble(ids, mine, other):
    half, share, piece, chans = mine.shape
    return kernel_call(
        assemble_kernel,
        [ids, mine, other],
        jax.ShapeDtypeStruct((share, 2 * half * piece, chans), jnp.float32),
        [],
        4,
        scalars=1,
    )


def reduced_gradient(ids, keep, send):
    n_lat, n_lon = lax.axis_size("lat"), lax.axis_size("lon")
    mask = 1
    while True:
        other = lax.ppermute(send, "lat", swap("lat", mask))
        total = keep + other.astype(jnp.float32)
        mask *= 2
        if mask >= n_lat:
            break
        half = total.shape[0] // 2
        keep, send = total[:half], total[half:].astype(jnp.bfloat16)
    total = total[0]
    wire = total.astype(jnp.bfloat16)
    piece = total[0]
    for s in range(1, n_lon):
        other = lax.ppermute(wire[s], "lon", ring("lon", s))
        piece = piece + other.astype(jnp.float32)
    pieces = piece.astype(jnp.bfloat16)[None]
    while mask > 1:
        mask //= 2
        other = lax.ppermute(pieces, "lat", swap("lat", mask))
        if mask > 1:
            pieces = jnp.concatenate([pieces, other], axis=0)
    return assemble(ids, pieces, other)


def on_device(field_in, quadrature, half_width, mixing, cotangent):
    rows, cols, chans = field_in.shape
    kernels, _, outs = mixing.shape
    taps = quadrature.shape[-1]
    rim = (taps - 1) // 2
    n_lat, n_lon = lax.axis_size("lat"), lax.axis_size("lon")
    ids = jnp.stack([lax.axis_index("lat"), lax.axis_index("lon")]).astype(jnp.int32)
    groups = split_rows(rows)
    outer = groups[0]

    def beside(pair):
        left = lax.ppermute(pair[0], "lon", ring("lon", 1))
        right = lax.ppermute(pair[1], "lon", ring("lon", -1))
        return [left, right]

    def bands_beside(pair):
        top = lax.ppermute(pair[0], "lat", line("lat", 1))
        bottom = lax.ppermute(pair[1], "lat", line("lat", -1))
        return top, bottom

    window = taps - 1 + BLOCK
    *sides, own_edges = rims(field_in, rim, groups)
    outer_sides = beside(sides[0:2])
    inner_sides = beside(sides[2:4])
    bands, basis_edges = band_matrices(half_width, quadrature)
    picks = (0, len(outer) - 1)
    sent = edge_rows(own_edges, *outer_sides, picks, [])
    f_top, f_bottom = bands_beside(sent)
    *sides, cot_edges = rims(cotangent, rim, [range(rows)])
    g_left, g_right = beside(sides)

    filtered, keep, send = forward(
        ids,
        bands,
        field_in,
        f_top,
        f_bottom,
        cotangent.reshape(rows * cols, outs),
        groups,
        outer_sides + inner_sides,
        kernels,
        n_lat,
        n_lon,
    )
    weight_grad = reduced_gradient(ids, keep, send)
    field_out = kernel_call(
        mix_kernel,
        [filtered, mixing.reshape(kernels * chans, outs)],
        jax.ShapeDtypeStruct((rows * cols, outs), jnp.bfloat16),
        [],
        8,
    )
    sent = edge_rows(cot_edges, g_left, g_right, (0, rows - 1), [basis_edges])
    g_top, g_bottom = bands_beside(sent)
    input_grad = backward_inner(bands, cotangent, mixing, g_left, g_right, window)
    near_edges = jnp.concatenate([cotangent[:2], cotangent[rows - 2 :]], axis=0)
    input_grad = backward_edges(
        bands, g_top, g_bottom, mixing, g_left, g_right, near_edges, input_grad, window
    )
    return (
        field_out.reshape(rows, cols, outs),
        input_grad,
        weight_grad,
    )


def solution(mesh):
    return jax.shard_map(
        on_device,
        mesh=mesh,
        in_specs=(
            P(("ens", "lat"), "lon", None),
            P("lat", None, None, None),
            P("lat"),
            P(),
            P(("ens", "lat"), "lon", None),
        ),
        out_specs=(
            P(("ens", "lat"), "lon", None),
            P(("ens", "lat"), "lon", None),
            P("lon", "ens", None),
        ),
        check_vma=False,
    )
```

```python
import functools

import jax
import jax.numpy as jnp
from jax import lax
from jax.experimental import pallas as pl
from jax.experimental.pallas import tpu as pltpu
from jax.sharding import PartitionSpec as P


BLOCK = 32
LANES = 128
DEPTH = 256


def ring(axis, distance):
    count = lax.axis_size(axis)
    return [(i, (i + distance) % count) for i in range(count)]


def line(axis, distance):
    count = lax.axis_size(axis)
    return [(i, i + distance) for i in range(count) if 0 <= i + distance < count]


def swap(axis, mask):
    return [(i, i ^ mask) for i in range(lax.axis_size(axis))]


IN_VMEM = pl.BlockSpec(memory_space=pltpu.VMEM)
IN_SMEM = pl.BlockSpec(memory_space=pltpu.SMEM)
IN_HBM = pl.BlockSpec(memory_space=pltpu.HBM)


def near(array):
    return pltpu.with_memory_space_constraint(array, pltpu.VMEM)


def kernel_call(body, operands, outs, scratch, mib, scalars=0, far=(), far_out=False, alias=None):
    specs = [IN_SMEM] * scalars
    given = [pltpu.with_memory_space_constraint(x, pltpu.HBM) for x in operands[:scalars]]
    for i, operand in enumerate(operands[scalars:], scalars):
        specs.append(IN_HBM if i in far else IN_VMEM)
        given.append(pltpu.with_memory_space_constraint(operand, pltpu.HBM) if i in far else near(operand))
    single = not isinstance(outs, list)
    place = IN_HBM if far_out else IN_VMEM
    return pl.pallas_call(
        body,
        in_specs=specs,
        out_specs=place if single else [place] * len(outs),
        out_shape=outs,
        scratch_shapes=scratch,
        input_output_aliases=alias or {},
        compiler_params=pltpu.CompilerParams(vmem_limit_bytes=mib << 20),
    )(*given)


def packed_taps(pieces, window, total):
    kernels = pieces[0].shape[0]
    packed = None
    for r, piece in enumerate(pieces):
        wide = jnp.concatenate([piece, jnp.zeros((kernels, total - piece.shape[1]), piece.dtype)], 1)
        wide = pltpu.roll(wide, r * window, 1) if r else wide
        packed = wide if packed is None else packed + wide
    return packed


def spread_bands(packed, bands, row):
    kernels, total = packed.shape
    for k in range(kernels):
        rows = jnp.broadcast_to(packed[k : k + 1, :], (BLOCK, total))
        rolled = pltpu.roll(rows, 0, 1, stride=1, stride_axis=0)
        bands[row, k * BLOCK : (k + 1) * BLOCK, :] = rolled.astype(bands.dtype)


def bands_kernel(reach, quadrature, field, cot, bands, edges, field_near, cot_near, sems):
    copies = [
        pltpu.make_async_copy(field, field_near, sems.at[0]),
        pltpu.make_async_copy(cot, cot_near, sems.at[1]),
    ]
    for copy in copies:
        copy.start()
    rows, three, kernels, taps = quadrature.shape
    window = taps - 1 + BLOCK
    middle = (taps - 1) // 2
    lane = lax.broadcasted_iota(jnp.int32, (kernels, LANES), 1)
    for row in range(rows):
        half = jnp.broadcast_to(reach[row : row + 1, :], (kernels, LANES))
        factor = 1.0 / jnp.sqrt(3.0 * (2.0 * half.astype(jnp.float32) + 1.0))
        head_inside = (jnp.abs(lane - middle) <= half).astype(jnp.float32)
        tail_inside = ((lane < taps - LANES) & (lane + LANES - middle <= half)).astype(jnp.float32)
        pieces = []
        for r in range(three):
            head = quadrature[row, r, :, 0:LANES] * factor * head_inside
            last = jnp.broadcast_to(quadrature[row, r, :, LANES:taps], (kernels, LANES))
            tail = last * factor * tail_inside
            piece = jnp.concatenate([head, tail], axis=1).astype(jnp.bfloat16)
            if row == rows - 1 and r == three - 1:
                edges[0] = piece
            if row == 0 and r == 0:
                edges[1] = piece
            pieces.append(piece.astype(jnp.float32))
        spread_bands(packed_taps(pieces, window, bands.shape[2]), bands, row)
    for copy in copies:
        copy.wait()


def band_matrices(reach, quadrature, field, cot):
    rows, three, kernels, taps = quadrature.shape
    total = -(-three * (taps - 1 + BLOCK) // DEPTH) * DEPTH
    return kernel_call(
        bands_kernel,
        [reach, quadrature, field, cot],
        [
            pltpu.VMEM((rows, kernels * BLOCK, total), jnp.bfloat16),
            pltpu.VMEM((2, kernels, 2 * LANES), jnp.bfloat16),
            pltpu.VMEM(field.shape, field.dtype),
            pltpu.VMEM(cot.shape, cot.dtype),
        ],
        [pltpu.SemaphoreType.DMA((2,))],
        10,
        far=(2, 3),
    )


def split_rows(rows):
    part = max(1, rows // 4)
    outer = list(range(part)) + list(range(rows - part, rows))
    return outer, list(range(part, rows - part))


def rim_copies(groups, array, outs, edges):
    rows, cols = array.shape[0], array.shape[1]
    rim = outs[0].shape[1]
    copies = []
    for g, group in enumerate(groups):
        place = 0
        while place < len(group):
            size = 1
            while place + size < len(group) and group[place + size] == group[place] + size:
                size += 1
            source = array.at[pl.ds(group[place], size)]
            for side, first in ((0, cols - rim), (1, 0)):
                target = outs[2 * g + side].at[pl.ds(place, size)]
                copies.append((source.at[:, pl.ds(first, rim), :], target))
            place += size
    copies.append((array.at[0], edges.at[0]))
    copies.append((array.at[rows - 1], edges.at[1]))
    return copies


def run_copies(copies, sems, between=None):
    copies = [pltpu.make_async_copy(*c, sems.at[i]) for i, c in enumerate(copies)]
    for copy in copies:
        copy.start()
    if between:
        between()
    for copy in copies:
        copy.wait()


def first_kernel(groups, half_width, array, quadrature, *refs):
    *outs, edges, taps_near, reach, sems = refs

    def spread_reach():
        for row in range(reach.shape[0]):
            reach[row : row + 1, :] = jnp.full((1, LANES), half_width[row], jnp.int32)

    copies = rim_copies(groups, array, outs, edges)
    run_copies(copies + [(quadrature, taps_near)], sems, spread_reach)


def rims_kernel(groups, array, *refs):
    *outs, edges, sems = refs
    run_copies(rim_copies(groups, array, outs, edges), sems)


def rim_shapes(array, rim, groups):
    _, cols, chans = array.shape
    outs = [
        pltpu.VMEM((len(group), rim, chans), jnp.bfloat16) for group in groups for _ in range(2)
    ]
    return outs + [pltpu.VMEM((2, cols, chans), jnp.bfloat16)]


def first_rims(half_width, array, quadrature, rim, groups):
    outs = rim_shapes(array, rim, groups)
    outs.append(pltpu.VMEM(quadrature.shape, jnp.float32))
    outs.append(pltpu.VMEM((half_width.shape[0], LANES), jnp.int32))
    return kernel_call(
        functools.partial(first_kernel, groups),
        [half_width, array, quadrature],
        outs,
        [pltpu.SemaphoreType.DMA((16,))],
        6,
        scalars=1,
        far=(1, 2),
    )


def rims(array, rim, groups):
    return kernel_call(
        functools.partial(rims_kernel, groups),
        [array],
        rim_shapes(array, rim, groups),
        [pltpu.SemaphoreType.DMA((16,))],
        4,
        far=(0,),
    )


def edges_kernel(picks, own, left, right, *rest):
    *basis, bottom_row, top_row = rest
    rim, cols = left.shape[1], own.shape[1]
    for i, out in ((1, bottom_row), (0, top_row)):
        out[0:rim] = left[picks[i]]
        out[rim : rim + cols] = own[i]
        out[rim + cols : 2 * rim + cols] = right[picks[i]]
        if basis:
            out[2 * rim + cols :] = basis[0][1 - i]


def edge_rows(own, left, right, picks, basis):
    _, cols, chans = own.shape
    span = cols + 2 * left.shape[1] + (basis[0].shape[1] if basis else 0)
    outs = [pltpu.VMEM((span, chans), jnp.bfloat16)] * 2
    return kernel_call(
        functools.partial(edges_kernel, picks), [own, left, right, *basis], outs, [], 4
    )


def fill_extended(ext, own, top, bottom, groups, sides):
    rows, cols = own.shape[0], own.shape[1]
    rim = sides[0].shape[1]
    span = ext.shape[1]
    ext[0] = top[0:span]
    ext[rows + 1] = bottom[0:span]
    ext[1 : rows + 1, rim : rim + cols, :] = own[...]
    for g, group in enumerate(groups):
        for i, row in enumerate(group):
            ext[row + 1, 0:rim, :] = sides[2 * g][i]
            ext[row + 1, rim + cols :, :] = sides[2 * g + 1][i]


def filter_rows(bands, ext, cols, write):
    rows, height, total = bands.shape
    reach = ext.shape[1] - cols + BLOCK
    spare = total - 3 * reach

    def one(row, carry):
        for g in range(cols // BLOCK):
            first = g * BLOCK
            pieces = [ext[row + r, first : first + reach, :] for r in range(3)]
            if spare:
                pieces.append(ext[row, 0:spare, :])
            source = jnp.concatenate(pieces, axis=0)
            result = jnp.dot(bands[row], source, preferred_element_type=jnp.float32)
            result = result.astype(jnp.bfloat16)
            start = pl.multiple_of(row * cols + first, BLOCK)
            for k in range(height // BLOCK):
                write(start, k, result[k * BLOCK : (k + 1) * BLOCK])
        return carry

    lax.fori_loop(0, rows, one, 0)


def forward_kernel(n_lat, groups, ids, bands, own, top, bottom, cot, *rest):
    *sides, filt, keep, send, ext, grad = rest
    _, cols, chans = own.shape
    kernels = grad.shape[0]
    fill_extended(ext, own, top, bottom, groups, sides)

    def write(start, k, value):
        filt[pl.ds(start, BLOCK), k * chans : (k + 1) * chans] = value

    filter_rows(bands, ext, cols, write)
    for k in range(kernels):
        grad[k] = lax.dot_general(
            filt[:, k * chans : (k + 1) * chans],
            cot[...],
            (((0,), (0,)), ((), ())),
            preferred_element_type=jnp.float32,
        )
    lat, lon = ids[0], ids[1]
    n_lon, share, piece = keep.shape[1], keep.shape[2], keep.shape[3]
    bits = n_lat.bit_length() - 1
    for m in range(n_lat):
        slot = sum(((m >> b) & 1) << (bits - 1 - b) for b in range(bits))
        start = pl.multiple_of((lat ^ slot) * piece, piece)
        for s in range(n_lon):
            first = lax.rem(lon + s, n_lon) * share
            value = grad[pl.ds(first, share), pl.ds(start, piece), :]
            if m < n_lat // 2:
                keep[m, s] = value
            else:
                send[m - n_lat // 2, s] = value.astype(send.dtype)


def forward(ids, bands, own, top, bottom, cot, groups, sides, kernels, n_lat, n_lon):
    rows, cols, chans = own.shape
    rim = sides[0].shape[1]
    parts = (n_lat // 2, n_lon, kernels // n_lon, chans // n_lat, chans)
    return kernel_call(
        functools.partial(forward_kernel, n_lat, groups),
        [ids, bands, own, top, bottom, cot, *sides],
        [
            pltpu.VMEM((rows * cols, kernels * chans), jnp.bfloat16),
            pltpu.VMEM(parts, jnp.float32),
            pltpu.VMEM(parts, jnp.bfloat16),
        ],
        [
            pltpu.VMEM((rows + 2, cols + 2 * rim, chans), jnp.bfloat16),
            pltpu.VMEM((kernels, chans, chans), jnp.float32),
        ],
        20,
        scalars=1,
    )


def mix_kernel(filt, mixing, out):
    out[...] = jnp.dot(filt[...], mixing[...], preferred_element_type=jnp.float32).astype(out.dtype)


def mirror(size):
    across = lax.broadcasted_iota(jnp.int32, (size, size), 0)
    down = lax.broadcasted_iota(jnp.int32, (size, size), 1)
    return (across + down == size - 1).astype(jnp.float32).astype(jnp.bfloat16)


def adjoint_band(window, above, here, below):
    total = here.shape[1]
    sources = [below, here, above]
    lane = lax.broadcasted_iota(jnp.int32, (here.shape[0], LANES), 1)
    tiles = []
    for first in range(0, total, LANES):
        r = min(first // window, 2)
        tile = sources[r][:, first : first + LANES]
        cut = (r + 1) * window - first
        if r < 2 and cut < LANES:
            following = sources[r + 1][:, first : first + LANES]
            tile = jnp.where(lane < cut, tile, following)
        tiles.append(tile)
    return jnp.concatenate(tiles, axis=1)


def adjoint_row(band, reversed_rows, cols, write):
    span = reversed_rows[0].shape[0]
    reach = span - cols + BLOCK
    spare = band.shape[1] - 3 * reach
    for g in range(cols // BLOCK):
        first = g * BLOCK
        pieces = [source[first : first + reach, :] for source in reversed_rows]
        if spare:
            pieces.append(reversed_rows[0][0:spare, :])
        result = jnp.dot(
            band, jnp.concatenate(pieces, axis=0), preferred_element_type=jnp.float32
        ).astype(jnp.bfloat16)
        for k in range(result.shape[0] // BLOCK):
            write(first, k, result[k * BLOCK : (k + 1) * BLOCK])


def backward_inner_kernel(window, bands, own, left, right, filt, reverse):
    rows, cols, _ = own.shape
    flip = mirror(reverse.shape[1])

    def turn(row, carry):
        line = jnp.concatenate([left[row], own[row], right[row]], axis=0)
        reverse[row] = jnp.dot(flip, line, preferred_element_type=jnp.float32).astype(
            reverse.dtype
        )
        return carry

    lax.fori_loop(0, rows, turn, 0)

    def one(step, carry):
        row = step + 1
        band = adjoint_band(window, bands[row - 1], bands[row], bands[row + 1])
        base = step * cols

        def write(first, k, value):
            filt[k, pl.ds(pl.multiple_of(base + first, BLOCK), BLOCK), :] = value

        lines = [reverse.at[row + 1], reverse.at[row], reverse.at[row - 1]]
        adjoint_row(band, lines, cols, write)
        return carry

    lax.fori_loop(0, rows - 2, one, 0)


def backward_inner(bands, own, left, right, window):
    rows, cols, outs = own.shape
    span = cols + 2 * left.shape[1]
    kernels = bands.shape[1] // BLOCK
    return kernel_call(
        functools.partial(backward_inner_kernel, window),
        [bands, own, left, right],
        pltpu.VMEM((kernels, (rows - 2) * cols, outs), jnp.bfloat16),
        [pltpu.VMEM((rows, span, outs), jnp.bfloat16)],
        12,
    )


def backward_edges_kernel(
    window, bands, top, bottom, mixing, left, right, own, inner, out, reverse, extra, filt
):
    rows, cols, _ = own.shape
    span = reverse.shape[1]
    flip = mirror(span)
    lines = [top[0:span]]
    for row in (0, 1, rows - 2, rows - 1):
        lines.append(jnp.concatenate([left[row], own[row], right[row]], axis=0))
    lines.append(bottom[0:span])
    for i, line in enumerate(lines):
        reverse[i] = jnp.dot(flip, line, preferred_element_type=jnp.float32).astype(reverse.dtype)
    none = jnp.zeros((top.shape[0] - span, 2 * LANES), jnp.float32)
    above = top[span:, :].astype(jnp.float32)
    below = bottom[span:, :].astype(jnp.float32)
    spread_bands(packed_taps([none, none, above], window, bands.shape[2]), extra, 0)
    spread_bands(packed_taps([below, none, none], window, bands.shape[2]), extra, 1)
    picks = (
        (extra[0], bands[0], bands[1], 1),
        (bands[rows - 2], bands[rows - 1], extra[1], 4),
    )
    for i, (one, two, three, at) in enumerate(picks):
        band = adjoint_band(window, one, two, three)

        def write(first, k, value, base=i * cols):
            filt[k, base + first : base + first + BLOCK, :] = value

        adjoint_row(band, [reverse.at[at + 1], reverse.at[at], reverse.at[at - 1]], cols, write)
    turned = mirror(cols)
    for source, where in ((inner, range(1, rows - 1)), (filt, (0, rows - 1))):
        total = None
        for k in range(mixing.shape[0]):
            term = lax.dot_general(
                source[k], mixing[k], (((1,), (1,)), ((), ())), preferred_element_type=jnp.float32
            )
            total = term if total is None else total + term
        total = total.astype(jnp.bfloat16)
        for i, row in enumerate(where):
            part = total[i * cols : (i + 1) * cols]
            part = jnp.dot(turned, part, preferred_element_type=jnp.float32)
            out[row] = part.astype(out.dtype)


def backward_edges(bands, top, bottom, mixing, left, right, own, inner, window):
    rows, cols, outs = own.shape
    span = cols + 2 * left.shape[1]
    kernels, chans, _ = mixing.shape
    return kernel_call(
        functools.partial(backward_edges_kernel, window),
        [bands, top, bottom, mixing, left, right, own, inner],
        jax.ShapeDtypeStruct((rows, cols, chans), jnp.bfloat16),
        [
            pltpu.VMEM((6, span, outs), jnp.bfloat16),
            pltpu.VMEM((2,) + bands.shape[1:], jnp.bfloat16),
            pltpu.VMEM((kernels, 2 * cols, outs), jnp.bfloat16),
        ],
        16,
    )


def assemble_kernel(ids, mine, other, out):
    half, _, piece, _ = mine.shape
    count = 2 * half
    bits = count.bit_length() - 1
    for slot in range(count):
        m = sum(((slot >> b) & 1) << (bits - 1 - b) for b in range(bits))
        source = mine[m] if m < half else other[m - half]
        start = pl.multiple_of((ids[0] ^ slot) * piece, piece)
        out[:, pl.ds(start, piece), :] = source.astype(out.dtype)


def assemble(ids, mine, other):
    half, share, piece, chans = mine.shape
    return kernel_call(
        assemble_kernel,
        [ids, mine, other],
        jax.ShapeDtypeStruct((share, 2 * half * piece, chans), jnp.float32),
        [],
        4,
        scalars=1,
    )


def reduced_gradient(ids, keep, send):
    n_lat, n_lon = lax.axis_size("lat"), lax.axis_size("lon")
    mask = 1
    while True:
        other = lax.ppermute(send, "lat", swap("lat", mask))
        total = keep + other.astype(jnp.float32)
        mask *= 2
        if mask >= n_lat:
            break
        half = total.shape[0] // 2
        keep, send = total[:half], total[half:].astype(jnp.bfloat16)
    total = total[0]
    wire = total.astype(jnp.bfloat16)
    piece = total[0]
    for s in range(1, n_lon):
        other = lax.ppermute(wire[s], "lon", ring("lon", s))
        piece = piece + other.astype(jnp.float32)
    pieces = piece.astype(jnp.bfloat16)[None]
    while mask > 1:
        mask //= 2
        other = lax.ppermute(pieces, "lat", swap("lat", mask))
        if mask > 1:
            pieces = jnp.concatenate([pieces, other], axis=0)
    return assemble(ids, pieces, other)


def on_device(field_in, quadrature, half_width, mixing, cotangent):
    rows, cols, chans = field_in.shape
    kernels, _, outs = mixing.shape
    taps = quadrature.shape[-1]
    rim = (taps - 1) // 2
    n_lat, n_lon = lax.axis_size("lat"), lax.axis_size("lon")
    ids = jnp.stack([lax.axis_index("lat"), lax.axis_index("lon")]).astype(jnp.int32)
    groups = split_rows(rows)
    outer = groups[0]

    def beside(pair):
        left = lax.ppermute(pair[0], "lon", ring("lon", 1))
        right = lax.ppermute(pair[1], "lon", ring("lon", -1))
        return [left, right]

    def bands_beside(pair):
        top = lax.ppermute(pair[0], "lat", line("lat", 1))
        bottom = lax.ppermute(pair[1], "lat", line("lat", -1))
        return top, bottom

    window = taps - 1 + BLOCK
    *sides, own_edges, taps_near, reach = first_rims(
        half_width, field_in, quadrature, rim, groups
    )
    outer_sides = beside(sides[0:2])
    inner_sides = beside(sides[2:4])
    bands, basis_edges, field_near, cot_near = band_matrices(
        reach, taps_near, field_in, cotangent
    )
    picks = (0, len(outer) - 1)
    sent = edge_rows(own_edges, *outer_sides, picks, [])
    f_top, f_bottom = bands_beside(sent)
    *sides, cot_edges = rims(cotangent, rim, [range(rows)])
    g_left, g_right = beside(sides)

    filtered, keep, send = forward(
        ids,
        bands,
        field_near,
        f_top,
        f_bottom,
        cot_near.reshape(rows * cols, outs),
        groups,
        outer_sides + inner_sides,
        kernels,
        n_lat,
        n_lon,
    )
    weight_grad = reduced_gradient(ids, keep, send)
    field_out = kernel_call(
        mix_kernel,
        [filtered, mixing.reshape(kernels * chans, outs)],
        jax.ShapeDtypeStruct((rows * cols, outs), jnp.bfloat16),
        [],
        8,
    )
    sent = edge_rows(cot_edges, g_left, g_right, (0, rows - 1), [basis_edges])
    g_top, g_bottom = bands_beside(sent)
    inner = backward_inner(bands, cot_near, g_left, g_right, window)
    input_grad = backward_edges(
        bands, g_top, g_bottom, mixing, g_left, g_right, cot_near, inner, window
    )
    return (
        field_out.reshape(rows, cols, outs),
        input_grad,
        weight_grad,
    )


def solution(mesh):
    return jax.shard_map(
        on_device,
        mesh=mesh,
        in_specs=(
            P(("ens", "lat"), "lon", None),
            P("lat", None, None, None),
            P("lat"),
            P(),
            P(("ens", "lat"), "lon", None),
        ),
        out_specs=(
            P(("ens", "lat"), "lon", None),
            P(("ens", "lat"), "lon", None),
            P("lon", "ens", None),
        ),
        check_vma=False,
    )
```

```python
import functools

import jax
import jax.numpy as jnp
from jax import lax
from jax.experimental import pallas as pl
from jax.experimental.pallas import tpu as pltpu
from jax.sharding import PartitionSpec as P


BLOCK = 32
LANES = 128
DEPTH = 256


def ring(axis, distance):
    count = lax.axis_size(axis)
    return [(i, (i + distance) % count) for i in range(count)]


def swap(axis, mask):
    return [(i, i ^ mask) for i in range(lax.axis_size(axis))]


IN_VMEM = pl.BlockSpec(memory_space=pltpu.VMEM)
IN_SMEM = pl.BlockSpec(memory_space=pltpu.SMEM)
IN_HBM = pl.BlockSpec(memory_space=pltpu.HBM)


def near(array):
    return pltpu.with_memory_space_constraint(array, pltpu.VMEM)


def kernel_call(body, operands, outs, scratch, mib, scalars=0, far=(), far_out=False, alias=None):
    specs = [IN_SMEM] * scalars
    given = [pltpu.with_memory_space_constraint(x, pltpu.HBM) for x in operands[:scalars]]
    for i, operand in enumerate(operands[scalars:], scalars):
        specs.append(IN_HBM if i in far else IN_VMEM)
        given.append(pltpu.with_memory_space_constraint(operand, pltpu.HBM) if i in far else near(operand))
    single = not isinstance(outs, list)
    place = IN_HBM if far_out else IN_VMEM
    return pl.pallas_call(
        body,
        in_specs=specs,
        out_specs=place if single else [place] * len(outs),
        out_shape=outs,
        scratch_shapes=scratch,
        input_output_aliases=alias or {},
        compiler_params=pltpu.CompilerParams(vmem_limit_bytes=mib << 20),
    )(*given)


def packed_taps(pieces, window, total):
    kernels = pieces[0].shape[0]
    packed = None
    for r, piece in enumerate(pieces):
        wide = jnp.concatenate([piece, jnp.zeros((kernels, total - piece.shape[1]), piece.dtype)], 1)
        wide = pltpu.roll(wide, r * window, 1) if r else wide
        packed = wide if packed is None else packed + wide
    return packed


def spread_bands(packed, bands, row):
    kernels, total = packed.shape
    for k in range(kernels):
        rows = jnp.broadcast_to(packed[k : k + 1, :], (BLOCK, total))
        rolled = pltpu.roll(rows, 0, 1, stride=1, stride_axis=0)
        bands[row, k * BLOCK : (k + 1) * BLOCK, :] = rolled.astype(bands.dtype)


def bands_kernel(reach, quadrature, field, cot, bands, edges, field_near, cot_near, sems):
    copies = [
        pltpu.make_async_copy(field, field_near, sems.at[0]),
        pltpu.make_async_copy(cot, cot_near, sems.at[1]),
    ]
    for copy in copies:
        copy.start()
    rows, three, kernels, taps = quadrature.shape
    window = taps - 1 + BLOCK
    middle = (taps - 1) // 2
    lane = lax.broadcasted_iota(jnp.int32, (kernels, LANES), 1)
    for row in range(rows):
        half = jnp.broadcast_to(reach[row : row + 1, :], (kernels, LANES))
        factor = 1.0 / jnp.sqrt(3.0 * (2.0 * half.astype(jnp.float32) + 1.0))
        head_inside = (jnp.abs(lane - middle) <= half).astype(jnp.float32)
        tail_inside = ((lane < taps - LANES) & (lane + LANES - middle <= half)).astype(jnp.float32)
        pieces = []
        for r in range(three):
            head = quadrature[row, r, :, 0:LANES] * factor * head_inside
            last = jnp.broadcast_to(quadrature[row, r, :, LANES:taps], (kernels, LANES))
            tail = last * factor * tail_inside
            piece = jnp.concatenate([head, tail], axis=1).astype(jnp.bfloat16)
            if row == rows - 1 and r == three - 1:
                edges[0] = piece
            if row == 0 and r == 0:
                edges[1] = piece
            pieces.append(piece.astype(jnp.float32))
        spread_bands(packed_taps(pieces, window, bands.shape[2]), bands, row)
    for copy in copies:
        copy.wait()


def band_matrices(reach, quadrature, field, cot):
    rows, three, kernels, taps = quadrature.shape
    total = -(-three * (taps - 1 + BLOCK) // DEPTH) * DEPTH
    return kernel_call(
        bands_kernel,
        [reach, quadrature, field, cot],
        [
            pltpu.VMEM((rows, kernels * BLOCK, total), jnp.bfloat16),
            pltpu.VMEM((2, kernels, 2 * LANES), jnp.bfloat16),
            pltpu.VMEM(field.shape, field.dtype),
            pltpu.VMEM(cot.shape, cot.dtype),
        ],
        [pltpu.SemaphoreType.DMA((2,))],
        10,
        far=(2, 3),
    )


def split_rows(rows):
    part = max(1, rows // 4)
    outer = list(range(part)) + list(range(rows - part, rows))
    return outer, list(range(part, rows - part))


def rim_copies(groups, array, outs, edges):
    rows, cols = array.shape[0], array.shape[1]
    rim = outs[0].shape[1]
    copies = []
    for g, group in enumerate(groups):
        place = 0
        while place < len(group):
            size = 1
            while place + size < len(group) and group[place + size] == group[place] + size:
                size += 1
            source = array.at[pl.ds(group[place], size)]
            for side, first in ((0, cols - rim), (1, 0)):
                target = outs[2 * g + side].at[pl.ds(place, size)]
                copies.append((source.at[:, pl.ds(first, rim), :], target))
            place += size
    copies.append((array.at[0], edges.at[0]))
    copies.append((array.at[rows - 1], edges.at[1]))
    return copies


def run_copies(copies, sems, between=None):
    copies = [pltpu.make_async_copy(*c, sems.at[i]) for i, c in enumerate(copies)]
    for copy in copies:
        copy.start()
    if between:
        between()
    for copy in copies:
        copy.wait()


def second_kernel(groups, half_width, array, quadrature, *refs):
    *outs, edges, taps_near, reach, widths, sems = refs
    first = pltpu.make_async_copy(half_width, widths, sems.at[15])
    first.start()

    def spread_reach():
        first.wait()
        for row in range(reach.shape[0]):
            reach[row : row + 1, :] = jnp.full((1, LANES), widths[row], jnp.int32)

    copies = rim_copies(groups, array, outs, edges)
    run_copies(copies + [(quadrature, taps_near)], sems, spread_reach)


def rims_kernel(groups, array, *refs):
    *outs, edges, sems = refs
    run_copies(rim_copies(groups, array, outs, edges), sems)


def rim_shapes(array, rim, groups):
    _, cols, chans = array.shape
    outs = [
        pltpu.VMEM((len(group), rim, chans), jnp.bfloat16) for group in groups for _ in range(2)
    ]
    return outs + [pltpu.VMEM((2, cols, chans), jnp.bfloat16)]


def second_rims(half_width, array, quadrature, rim, groups):
    outs = rim_shapes(array, rim, groups)
    outs.append(pltpu.VMEM(quadrature.shape, jnp.float32))
    outs.append(pltpu.VMEM((half_width.shape[0], LANES), jnp.int32))
    return kernel_call(
        functools.partial(second_kernel, groups),
        [half_width, array, quadrature],
        outs,
        [pltpu.SMEM(half_width.shape, jnp.int32), pltpu.SemaphoreType.DMA((16,))],
        6,
        far=(0, 1, 2),
    )


def rims(array, rim, groups):
    return kernel_call(
        functools.partial(rims_kernel, groups),
        [array],
        rim_shapes(array, rim, groups),
        [pltpu.SemaphoreType.DMA((16,))],
        4,
        far=(0,),
    )


def even_band():
    return lax.rem(lax.axis_index("lat"), 2) == 0


def edges_kernel(picks, own, left, right, *rest):
    *basis, core_row, far_row = rest
    rim, cols = left.shape[1], own.shape[1]
    even = even_band()
    for out, last in ((core_row, even), (far_row, jnp.logical_not(even))):
        i = jnp.where(last, 1, 0)
        pick = jnp.where(last, picks[1], picks[0])
        out[0:rim] = left[pick]
        out[rim : rim + cols] = own[i]
        out[rim + cols : 2 * rim + cols] = right[pick]
        if basis:
            out[2 * rim + cols :] = basis[0][1 - i]


def edge_rows(own, left, right, picks, basis):
    _, cols, chans = own.shape
    span = cols + 2 * left.shape[1] + (basis[0].shape[1] if basis else 0)
    outs = [pltpu.VMEM((span, chans), jnp.bfloat16)] * 2
    return kernel_call(
        functools.partial(edges_kernel, picks), [own, left, right, *basis], outs, [], 4
    )


def fill_extended(ext, own, core, far, groups, sides):
    rows, cols = own.shape[0], own.shape[1]
    rim = sides[0].shape[1]
    span = ext.shape[1]
    even = even_band()
    ext[jnp.where(even, rows + 1, 0)] = core[0:span]
    ext[jnp.where(even, 0, rows + 1)] = far[0:span]
    ext[1 : rows + 1, rim : rim + cols, :] = own[...]
    for g, group in enumerate(groups):
        for i, row in enumerate(group):
            ext[row + 1, 0:rim, :] = sides[2 * g][i]
            ext[row + 1, rim + cols :, :] = sides[2 * g + 1][i]


def filter_rows(bands, ext, cols, write):
    rows, height, total = bands.shape
    reach = ext.shape[1] - cols + BLOCK
    spare = total - 3 * reach
    for row in range(rows):
        for first in range(0, cols, BLOCK):
            pieces = [ext[row + r, first : first + reach, :] for r in range(3)]
            if spare:
                pieces.append(ext[row, 0:spare, :])
            source = jnp.concatenate(pieces, axis=0)
            result = jnp.dot(bands[row], source, preferred_element_type=jnp.float32)
            result = result.astype(jnp.bfloat16)
            for k in range(height // BLOCK):
                write(row * cols + first, k, result[k * BLOCK : (k + 1) * BLOCK])


def forward_kernel(groups, bands, own, core, far, cot, *rest):
    *sides, filt, keep, send, ext, grad = rest
    _, cols, chans = own.shape
    kernels = grad.shape[0]
    fill_extended(ext, own, core, far, groups, sides)

    def write(start, k, value):
        filt[start : start + BLOCK, k * chans : (k + 1) * chans] = value

    filter_rows(bands, ext, cols, write)
    for k in range(kernels):
        grad[k] = lax.dot_general(
            filt[:, k * chans : (k + 1) * chans],
            cot[...],
            (((0,), (0,)), ((), ())),
            preferred_element_type=jnp.float32,
        )
    lat, lon = lax.axis_index("lat"), lax.axis_index("lon")
    n_lon, share, piece = keep.shape[0], keep.shape[1], keep.shape[2]
    for slot, out in ((0, keep), (1, send)):
        start = pl.multiple_of((lax.rem(lat, 2) ^ slot) * piece, piece)
        for s in range(n_lon):
            first = lax.rem(lon + s, n_lon) * share
            value = grad[pl.ds(first, share), pl.ds(start, piece), :]
            out[s] = value.astype(out.dtype)


def forward(bands, own, core, far, cot, groups, sides, kernels, n_lon):
    rows, cols, chans = own.shape
    rim = sides[0].shape[1]
    parts = (n_lon, kernels // n_lon, chans // 2, cot.shape[1])
    return kernel_call(
        functools.partial(forward_kernel, groups),
        [bands, own, core, far, cot, *sides],
        [
            pltpu.VMEM((rows * cols, kernels * chans), jnp.bfloat16),
            pltpu.VMEM(parts, jnp.float32),
            pltpu.VMEM(parts, jnp.bfloat16),
        ],
        [
            pltpu.VMEM((rows + 2, cols + 2 * rim, chans), jnp.bfloat16),
            pltpu.VMEM((kernels, chans, chans), jnp.float32),
        ],
        20,
    )


def mix_kernel(filt, mixing, out):
    out[...] = jnp.dot(filt[...], mixing[...], preferred_element_type=jnp.float32).astype(out.dtype)


def mirror(size):
    across = lax.broadcasted_iota(jnp.int32, (size, size), 0)
    down = lax.broadcasted_iota(jnp.int32, (size, size), 1)
    return (across + down == size - 1).astype(jnp.float32).astype(jnp.bfloat16)


def adjoint_band(window, above, here, below):
    total = here.shape[1]
    sources = [below, here, above]
    lane = lax.broadcasted_iota(jnp.int32, (here.shape[0], LANES), 1)
    tiles = []
    for first in range(0, total, LANES):
        r = min(first // window, 2)
        tile = sources[r][:, first : first + LANES]
        cut = (r + 1) * window - first
        if r < 2 and cut < LANES:
            following = sources[r + 1][:, first : first + LANES]
            tile = jnp.where(lane < cut, tile, following)
        tiles.append(tile)
    return jnp.concatenate(tiles, axis=1)


def adjoint_row(band, reversed_rows, cols, write):
    span = reversed_rows[0].shape[0]
    reach = span - cols + BLOCK
    spare = band.shape[1] - 3 * reach
    for g in range(cols // BLOCK):
        first = g * BLOCK
        pieces = [source[first : first + reach, :] for source in reversed_rows]
        if spare:
            pieces.append(reversed_rows[0][0:spare, :])
        result = jnp.dot(
            band, jnp.concatenate(pieces, axis=0), preferred_element_type=jnp.float32
        ).astype(jnp.bfloat16)
        for k in range(result.shape[0] // BLOCK):
            write(first, k, result[k * BLOCK : (k + 1) * BLOCK])


def backward_inner_kernel(window, bands, own, left, right, filt, reverse):
    rows, cols, _ = own.shape
    flip = mirror(reverse.shape[1])

    for row in range(rows):
        line = jnp.concatenate([left[row], own[row], right[row]], axis=0)
        reverse[row] = jnp.dot(flip, line, preferred_element_type=jnp.float32).astype(
            reverse.dtype
        )
    for row in range(1, rows - 1):
        band = adjoint_band(window, bands[row - 1], bands[row], bands[row + 1])

        def write(first, k, value, base=(row - 1) * cols):
            filt[k, base + first : base + first + BLOCK, :] = value

        lines = [reverse.at[row + 1], reverse.at[row], reverse.at[row - 1]]
        adjoint_row(band, lines, cols, write)


def backward_inner(bands, own, left, right, window):
    rows, cols, outs = own.shape
    span = cols + 2 * left.shape[1]
    kernels = bands.shape[1] // BLOCK
    return kernel_call(
        functools.partial(backward_inner_kernel, window),
        [bands, own, left, right],
        pltpu.VMEM((kernels, (rows - 2) * cols, outs), jnp.bfloat16),
        [pltpu.VMEM((rows, span, outs), jnp.bfloat16)],
        12,
    )


def backward_edges_kernel(
    window, bands, core, far, mixing, left, right, own, inner, out, reverse, extra, filt
):
    rows, cols, _ = own.shape
    span = reverse.shape[1]
    flip = mirror(span)
    even = even_band()
    lines = [(jnp.where(even, 5, 0), core[0:span]), (jnp.where(even, 0, 5), far[0:span])]
    for i, row in enumerate((0, 1, rows - 2, rows - 1)):
        lines.append((i + 1, jnp.concatenate([left[row], own[row], right[row]], axis=0)))
    for i, line in lines:
        reverse[i] = jnp.dot(flip, line, preferred_element_type=jnp.float32).astype(reverse.dtype)
    none = jnp.zeros((core.shape[0] - span, 2 * LANES), jnp.float32)
    beside, across = core[span:, :].astype(jnp.float32), far[span:, :].astype(jnp.float32)
    above, below = jnp.where(even, across, beside), jnp.where(even, beside, across)
    spread_bands(packed_taps([none, none, above], window, bands.shape[2]), extra, 0)
    spread_bands(packed_taps([below, none, none], window, bands.shape[2]), extra, 1)
    picks = (
        (extra[0], bands[0], bands[1], 1),
        (bands[rows - 2], bands[rows - 1], extra[1], 4),
    )
    for i, (one, two, three, at) in enumerate(picks):
        band = adjoint_band(window, one, two, three)

        def write(first, k, value, base=i * cols):
            filt[k, base + first : base + first + BLOCK, :] = value

        adjoint_row(band, [reverse.at[at + 1], reverse.at[at], reverse.at[at - 1]], cols, write)
    turned = mirror(cols)
    for source, where in ((inner, range(1, rows - 1)), (filt, (0, rows - 1))):
        total = None
        for k in range(mixing.shape[0]):
            term = lax.dot_general(
                source[k], mixing[k], (((1,), (1,)), ((), ())), preferred_element_type=jnp.float32
            )
            total = term if total is None else total + term
        total = total.astype(jnp.bfloat16)
        for i, row in enumerate(where):
            part = total[i * cols : (i + 1) * cols]
            part = jnp.dot(turned, part, preferred_element_type=jnp.float32)
            out[row] = part.astype(out.dtype)


def backward_edges(bands, core, far, mixing, left, right, own, inner, window):
    rows, cols, outs = own.shape
    span = cols + 2 * left.shape[1]
    kernels, chans, _ = mixing.shape
    return kernel_call(
        functools.partial(backward_edges_kernel, window),
        [bands, core, far, mixing, left, right, own, inner],
        jax.ShapeDtypeStruct((rows, cols, chans), jnp.bfloat16),
        [
            pltpu.VMEM((6, span, outs), jnp.bfloat16),
            pltpu.VMEM((2,) + bands.shape[1:], jnp.bfloat16),
            pltpu.VMEM((kernels, 2 * cols, outs), jnp.bfloat16),
        ],
        16,
    )


def assemble_kernel(mine, other, out):
    _, piece, _ = mine.shape
    for slot, source in ((0, mine), (1, other)):
        start = pl.multiple_of((lax.rem(lax.axis_index("lat"), 2) ^ slot) * piece, piece)
        out[:, pl.ds(start, piece), :] = source[...].astype(out.dtype)


def assemble(mine, other):
    share, piece, chans = mine.shape
    return kernel_call(
        assemble_kernel,
        [mine, other],
        jax.ShapeDtypeStruct((share, 2 * piece, chans), jnp.float32),
        [],
        4,
    )


def reduced_gradient(keep, send):
    n_lat, n_lon = lax.axis_size("lat"), lax.axis_size("lon")
    total = keep + lax.ppermute(send, "lat", swap("lat", 1)).astype(jnp.float32)
    wire = total.astype(jnp.bfloat16)
    piece = total[0]
    for s in range(1, n_lon):
        other = lax.ppermute(wire[s], "lon", ring("lon", s))
        piece = piece + other.astype(jnp.float32)
    mask = 2
    while mask < n_lat:
        mine = piece.astype(jnp.bfloat16)
        other = lax.ppermute(mine, "lat", swap("lat", mask))
        piece = mine.astype(jnp.float32) + other.astype(jnp.float32)
        mask *= 2
    mine = piece.astype(jnp.bfloat16)
    return assemble(mine, lax.ppermute(mine, "lat", swap("lat", 1)))


def on_device(field_in, quadrature, half_width, mixing, cotangent):
    rows, cols, chans = field_in.shape
    kernels, _, outs = mixing.shape
    taps = quadrature.shape[-1]
    rim = (taps - 1) // 2
    n_lon = lax.axis_size("lon")
    groups = split_rows(rows)
    outer = groups[0]

    def beside(pair):
        left = lax.ppermute(pair[0], "lon", ring("lon", 1))
        right = lax.ppermute(pair[1], "lon", ring("lon", -1))
        return [left, right]

    def bands_beside(pair):
        across = [(i, i + 1) for i in range(1, lax.axis_size("lat") - 1, 2)]
        far = lax.ppermute(pair[1], "lat", across + [(j, i) for i, j in across])
        core = lax.ppermute(pair[0], "lat", swap("lat", 1))
        return core, far

    window = taps - 1 + BLOCK
    *sides, own_edges = rims(field_in, rim, groups)
    outer_sides = beside(sides[0:2])
    inner_sides = beside(sides[2:4])
    *sides, cot_edges, taps_near, reach = second_rims(
        half_width, cotangent, quadrature, rim, [range(rows)]
    )
    bands, basis_edges, field_near, cot_near = band_matrices(
        reach, taps_near, field_in, cotangent
    )
    picks = (0, len(outer) - 1)
    sent = edge_rows(own_edges, *outer_sides, picks, [])
    f_core, f_far = bands_beside(sent)
    g_left, g_right = beside(sides)

    filtered, keep, send = forward(
        bands,
        field_near,
        f_core,
        f_far,
        cot_near.reshape(rows * cols, outs),
        groups,
        outer_sides + inner_sides,
        kernels,
        n_lon,
    )
    weight_grad = reduced_gradient(keep, send)
    field_out = kernel_call(
        mix_kernel,
        [filtered, mixing.reshape(kernels * chans, outs)],
        jax.ShapeDtypeStruct((rows * cols, outs), jnp.bfloat16),
        [],
        8,
    )
    sent = edge_rows(cot_edges, g_left, g_right, (0, rows - 1), [basis_edges])
    g_core, g_far = bands_beside(sent)
    inner = backward_inner(bands, cot_near, g_left, g_right, window)
    input_grad = backward_edges(
        bands, g_core, g_far, mixing, g_left, g_right, cot_near, inner, window
    )
    return (
        field_out.reshape(rows, cols, outs),
        input_grad,
        weight_grad,
    )


def solution(mesh):
    return jax.shard_map(
        on_device,
        mesh=mesh,
        in_specs=(
            P(("ens", "lat"), "lon", None),
            P("lat", None, None, None),
            P("lat"),
            P(),
            P(("ens", "lat"), "lon", None),
        ),
        out_specs=(
            P(("ens", "lat"), "lon", None),
            P(("ens", "lat"), "lon", None),
            P("lon", "ens", None),
        ),
        check_vma=False,
    )
```

```python
import functools

import jax
import jax.numpy as jnp
from jax import lax
from jax.experimental import pallas as pl
from jax.experimental.pallas import tpu as pltpu
from jax.sharding import PartitionSpec as P


BLOCK = 32
LANES = 128
DEPTH = 256


def swap(axis, mask):
    return [(i, i ^ mask) for i in range(lax.axis_size(axis))]


IN_VMEM = pl.BlockSpec(memory_space=pltpu.VMEM)
IN_SMEM = pl.BlockSpec(memory_space=pltpu.SMEM)
IN_HBM = pl.BlockSpec(memory_space=pltpu.HBM)


def near(array):
    return pltpu.with_memory_space_constraint(array, pltpu.VMEM)


def kernel_call(body, operands, outs, scratch, mib, scalars=0, far=(), far_out=False, alias=None):
    specs = [IN_SMEM] * scalars
    given = [pltpu.with_memory_space_constraint(x, pltpu.HBM) for x in operands[:scalars]]
    for i, operand in enumerate(operands[scalars:], scalars):
        specs.append(IN_HBM if i in far else IN_VMEM)
        given.append(pltpu.with_memory_space_constraint(operand, pltpu.HBM) if i in far else near(operand))
    single = not isinstance(outs, list)
    place = IN_HBM if far_out else IN_VMEM
    return pl.pallas_call(
        body,
        in_specs=specs,
        out_specs=place if single else [place] * len(outs),
        out_shape=outs,
        scratch_shapes=scratch,
        input_output_aliases=alias or {},
        compiler_params=pltpu.CompilerParams(vmem_limit_bytes=mib << 20),
    )(*given)


def packed_taps(pieces, window, total):
    kernels = pieces[0].shape[0]
    packed = None
    for r, piece in enumerate(pieces):
        wide = jnp.concatenate([piece, jnp.zeros((kernels, total - piece.shape[1]), piece.dtype)], 1)
        wide = pltpu.roll(wide, r * window, 1) if r else wide
        packed = wide if packed is None else packed + wide
    return packed


def spread_bands(packed, bands, row):
    kernels, total = packed.shape
    for k in range(kernels):
        rows = jnp.broadcast_to(packed[k : k + 1, :], (BLOCK, total))
        rolled = pltpu.roll(rows, 0, 1, stride=1, stride_axis=0)
        bands[row, k * BLOCK : (k + 1) * BLOCK, :] = rolled.astype(bands.dtype)


def bands_kernel(reach, quadrature, bands, edges):
    rows, three, kernels, taps = quadrature.shape
    window = taps - 1 + BLOCK
    middle = (taps - 1) // 2
    lane = lax.broadcasted_iota(jnp.int32, (kernels, LANES), 1)
    for row in range(rows):
        half = jnp.broadcast_to(reach[row : row + 1, :], (kernels, LANES))
        factor = 1.0 / jnp.sqrt(3.0 * (2.0 * half.astype(jnp.float32) + 1.0))
        head_inside = (jnp.abs(lane - middle) <= half).astype(jnp.float32)
        tail_inside = ((lane < taps - LANES) & (lane + LANES - middle <= half)).astype(jnp.float32)
        pieces = []
        for r in range(three):
            head = quadrature[row, r, :, 0:LANES] * factor * head_inside
            last = jnp.broadcast_to(quadrature[row, r, :, LANES:taps], (kernels, LANES))
            tail = last * factor * tail_inside
            piece = jnp.concatenate([head, tail], axis=1).astype(jnp.bfloat16)
            if row == rows - 1 and r == three - 1:
                edges[0] = piece
            if row == 0 and r == 0:
                edges[1] = piece
            pieces.append(piece.astype(jnp.float32))
        spread_bands(packed_taps(pieces, window, bands.shape[2]), bands, row)


def band_matrices(reach, quadrature):
    rows, three, kernels, taps = quadrature.shape
    total = -(-three * (taps - 1 + BLOCK) // DEPTH) * DEPTH
    return kernel_call(
        bands_kernel,
        [reach, quadrature],
        [
            pltpu.VMEM((rows, kernels * BLOCK, total), jnp.bfloat16),
            pltpu.VMEM((2, kernels, 2 * LANES), jnp.bfloat16),
        ],
        [],
        8,
    )


def split_rows(rows):
    part = 1
    outer = list(range(part)) + list(range(rows - part, rows))
    return outer, list(range(part, rows - part))


def even_sector():
    return lax.rem(lax.axis_index("lon"), 2) == 0


def rim_places(cols, rim):
    even = even_sector()
    first = pl.multiple_of(jnp.where(even, rim + cols, 0), rim)
    second = pl.multiple_of(jnp.where(even, 0, rim + cols), rim)
    return first, second


def rim_copies(groups, array, outs):
    cols = array.shape[1]
    rim = outs[0].shape[1]
    even = even_sector()
    starts = (jnp.where(even, cols - rim, 0), jnp.where(even, 0, cols - rim))
    copies = []
    for g, group in enumerate(groups):
        place = 0
        while place < len(group):
            size = 1
            while place + size < len(group) and group[place + size] == group[place] + size:
                size += 1
            source = array.at[pl.ds(group[place], size)]
            for side, first in enumerate(starts):
                target = outs[2 * g + side].at[pl.ds(place, size)]
                first = pl.multiple_of(first, rim)
                copies.append((source.at[:, pl.ds(first, rim), :], target))
            place += size
    return copies


def rims_kernel(groups, field, *refs):
    *sides, sems = refs
    copies = rim_copies(groups, field, sides)
    copies = [pltpu.make_async_copy(*c, sems.at[i]) for i, c in enumerate(copies)]
    for copy in copies:
        copy.start()
    for copy in copies:
        copy.wait()


def rims(field, rim, groups):
    chans = field.shape[2]
    outs = [
        pltpu.VMEM((len(group), rim, chans), jnp.bfloat16) for group in groups for _ in range(2)
    ]
    return kernel_call(
        functools.partial(rims_kernel, groups),
        [field],
        outs,
        [pltpu.SemaphoreType.DMA((16,))],
        4,
        far=(0,),
    )


def loads_kernel(field, cot, quadrature, half_width, *refs):
    *sides, field_near, cot_near, taps_near, reach, widths, sems = refs
    first = pltpu.make_async_copy(half_width, widths, sems.at[0])
    first.start()
    copies = rim_copies([range(cot.shape[0])], cot, sides)
    copies += [(quadrature, taps_near), (field, field_near), (cot, cot_near)]
    copies = [pltpu.make_async_copy(*c, sems.at[i + 1]) for i, c in enumerate(copies)]
    for copy in copies:
        copy.start()
    first.wait()
    for row in range(reach.shape[0]):
        reach[row : row + 1, :] = jnp.full((1, LANES), widths[row], jnp.int32)
    for copy in copies:
        copy.wait()


def loads(field, cot, quadrature, half_width, rim):
    rows, _, chans = field.shape
    outs = [pltpu.VMEM((rows, rim, chans), jnp.bfloat16)] * 2
    outs.append(pltpu.VMEM(field.shape, field.dtype))
    outs.append(pltpu.VMEM(cot.shape, cot.dtype))
    outs.append(pltpu.VMEM(quadrature.shape, jnp.float32))
    outs.append(pltpu.VMEM((rows, LANES), jnp.int32))
    return kernel_call(
        loads_kernel,
        [field, cot, quadrature, half_width],
        outs,
        [pltpu.SMEM(half_width.shape, jnp.int32), pltpu.SemaphoreType.DMA((8,))],
        8,
        far=(0, 1, 2, 3),
    )


def even_band():
    return lax.rem(lax.axis_index("lat"), 2) == 0


def edges_kernel(picks, own, paired, other, *rest):
    *basis, core_row, far_row = rest
    rim, cols = paired.shape[1], own.shape[1]
    even = even_band()
    first, second = rim_places(cols, rim)
    for out, last in ((core_row, even), (far_row, jnp.logical_not(even))):
        pick = jnp.where(last, picks[1], picks[0])
        out[pl.ds(first, rim)] = paired[pick]
        out[pl.ds(second, rim)] = other[pick]
        out[rim : rim + cols] = own[jnp.where(last, own.shape[0] - 1, 0)]
        if basis:
            out[2 * rim + cols :] = basis[0][jnp.where(last, 0, 1)]


def edge_rows(own, paired, other, picks, basis):
    _, cols, chans = own.shape
    span = cols + 2 * paired.shape[1] + (basis[0].shape[1] if basis else 0)
    outs = [pltpu.VMEM((span, chans), jnp.bfloat16)] * 2
    return kernel_call(
        functools.partial(edges_kernel, picks), [own, paired, other, *basis], outs, [], 4
    )


def fill_extended(ext, own, core, far, groups, sides):
    rows, cols = own.shape[0], own.shape[1]
    rim = sides[0].shape[1]
    span = ext.shape[1]
    even = even_band()
    ext[jnp.where(even, rows + 1, 0)] = core[0:span]
    ext[jnp.where(even, 0, rows + 1)] = far[0:span]
    ext[1 : rows + 1, rim : rim + cols, :] = own[...]
    first, second = rim_places(cols, rim)
    for g, group in enumerate(groups):
        for i, row in enumerate(group):
            ext[row + 1, pl.ds(first, rim), :] = sides[2 * g][i]
            ext[row + 1, pl.ds(second, rim), :] = sides[2 * g + 1][i]


def filter_rows(bands, ext, cols, write):
    rows, height, total = bands.shape
    reach = ext.shape[1] - cols + BLOCK
    spare = total - 3 * reach
    for row in range(rows):
        for first in range(0, cols, BLOCK):
            pieces = [ext[row + r, first : first + reach, :] for r in range(3)]
            if spare:
                pieces.append(ext[row, 0:spare, :])
            source = jnp.concatenate(pieces, axis=0)
            result = jnp.dot(bands[row], source, preferred_element_type=jnp.float32)
            result = result.astype(jnp.bfloat16)
            for k in range(height // BLOCK):
                write(row * cols + first, k, result[k * BLOCK : (k + 1) * BLOCK])


def band_place(n_lat):
    bits = n_lat.bit_length() - 1
    lat = lax.axis_index("lat")
    return sum(((lat >> b) & 1) << (bits - 1 - b) for b in range(bits))


def half_gradient(n_lat, filt, cot, out, grad, slot):
    kernels, half, _ = grad.shape
    n_lon, share, piece = out.shape[1], out.shape[2], out.shape[3]
    place, lon = band_place(n_lat), lax.axis_index("lon")
    group = n_lat // 2
    side = pl.multiple_of(((place // group) ^ slot) * half, half)
    for k in range(kernels):
        grad[k] = lax.dot_general(
            filt[:, pl.ds(side + 2 * half * k, half)],
            cot[...],
            (((0,), (0,)), ((), ())),
            preferred_element_type=jnp.float32,
        )
    for m in range(group):
        start = pl.multiple_of(((place ^ m) % group) * piece, piece)
        for s in range(n_lon):
            first = (lon ^ s) * share
            out[m, s] = grad[pl.ds(first, share), pl.ds(start, piece), :].astype(out.dtype)


def forward_kernel(n_lat, groups, bands, own, core, far, cot, *rest):
    *sides, filt, send, ext, grad = rest
    _, cols, chans = own.shape
    fill_extended(ext, own, core, far, groups, sides)

    def write(start, k, value):
        filt[start : start + BLOCK, k * chans : (k + 1) * chans] = value

    filter_rows(bands, ext, cols, write)
    half_gradient(n_lat, filt, cot, send, grad, 1)


def part_shape(kernels, chans, outs, n_lat, n_lon):
    return (n_lat // 2, n_lon, kernels // n_lon, chans // n_lat, outs)


def forward(bands, own, core, far, cot, groups, sides, kernels, n_lat, n_lon):
    rows, cols, chans = own.shape
    outs = cot.shape[1]
    rim = sides[0].shape[1]
    return kernel_call(
        functools.partial(forward_kernel, n_lat, groups),
        [bands, own, core, far, cot, *sides],
        [
            pltpu.VMEM((rows * cols, kernels * chans), jnp.bfloat16),
            pltpu.VMEM(part_shape(kernels, chans, outs, n_lat, n_lon), jnp.bfloat16),
        ],
        [
            pltpu.VMEM((rows + 2, cols + 2 * rim, chans), jnp.bfloat16),
            pltpu.VMEM((kernels, chans // 2, outs), jnp.float32),
        ],
        20,
    )


def kept_kernel(n_lat, filt, cot, keep, grad):
    half_gradient(n_lat, filt, cot, keep, grad, 0)


def kept(filt, cot, kernels, n_lat, n_lon):
    chans, outs = filt.shape[1] // kernels, cot.shape[1]
    return kernel_call(
        functools.partial(kept_kernel, n_lat),
        [filt, cot],
        pltpu.VMEM(part_shape(kernels, chans, outs, n_lat, n_lon), jnp.float32),
        [pltpu.VMEM((kernels, chans // 2, outs), jnp.float32)],
        12,
    )


def mix_kernel(filt, mixing, out):
    out[...] = jnp.dot(filt[...], mixing[...], preferred_element_type=jnp.float32).astype(out.dtype)


def mirror(size):
    across = lax.broadcasted_iota(jnp.int32, (size, size), 0)
    down = lax.broadcasted_iota(jnp.int32, (size, size), 1)
    return (across + down == size - 1).astype(jnp.float32).astype(jnp.bfloat16)


def adjoint_band(window, above, here, below):
    total = here.shape[1]
    sources = [below, here, above]
    lane = lax.broadcasted_iota(jnp.int32, (here.shape[0], LANES), 1)
    tiles = []
    for first in range(0, total, LANES):
        r = min(first // window, 2)
        tile = sources[r][:, first : first + LANES]
        cut = (r + 1) * window - first
        if r < 2 and cut < LANES:
            following = sources[r + 1][:, first : first + LANES]
            tile = jnp.where(lane < cut, tile, following)
        tiles.append(tile)
    return jnp.concatenate(tiles, axis=1)


def adjoint_row(band, reversed_rows, cols, write):
    span = reversed_rows[0].shape[0]
    reach = span - cols + BLOCK
    spare = band.shape[1] - 3 * reach
    for g in range(cols // BLOCK):
        first = g * BLOCK
        pieces = [source[first : first + reach, :] for source in reversed_rows]
        if spare:
            pieces.append(reversed_rows[0][0:spare, :])
        result = jnp.dot(
            band, jnp.concatenate(pieces, axis=0), preferred_element_type=jnp.float32
        ).astype(jnp.bfloat16)
        for k in range(result.shape[0] // BLOCK):
            write(first, k, result[k * BLOCK : (k + 1) * BLOCK])


def backward_inner_kernel(window, bands, own, paired, other, filt, reverse, lines):
    rows, cols, _ = own.shape
    rim = paired.shape[1]
    flip = mirror(reverse.shape[1])
    first, second = rim_places(cols, rim)
    for row in range(rows):
        lines[row, pl.ds(first, rim), :] = paired[row]
        lines[row, pl.ds(second, rim), :] = other[row]
        lines[row, rim : rim + cols, :] = own[row]
    for row in range(rows):
        reverse[row] = jnp.dot(flip, lines[row], preferred_element_type=jnp.float32).astype(
            reverse.dtype
        )
    for row in range(1, rows - 1):
        band = adjoint_band(window, bands[row - 1], bands[row], bands[row + 1])

        def write(first, k, value, base=(row - 1) * cols):
            filt[k, base + first : base + first + BLOCK, :] = value

        lines = [reverse.at[row + 1], reverse.at[row], reverse.at[row - 1]]
        adjoint_row(band, lines, cols, write)


def backward_inner(bands, own, paired, other, window):
    rows, cols, outs = own.shape
    span = cols + 2 * paired.shape[1]
    kernels = bands.shape[1] // BLOCK
    return kernel_call(
        functools.partial(backward_inner_kernel, window),
        [bands, own, paired, other],
        [
            pltpu.VMEM((kernels, (rows - 2) * cols, outs), jnp.bfloat16),
            pltpu.VMEM((rows, span, outs), jnp.bfloat16),
        ],
        [pltpu.VMEM((rows, span, outs), jnp.bfloat16)],
        12,
    )


def backward_edges_kernel(
    window, cols, bands, core, far, turned, filt, edge, extra
):
    rows, span, _ = turned.shape
    flip = mirror(span)
    even = even_band()
    for i, line in ((jnp.where(even, 1, 0), core), (jnp.where(even, 0, 1), far)):
        edge[i] = jnp.dot(flip, line[0:span], preferred_element_type=jnp.float32).astype(edge.dtype)
    none = jnp.zeros((core.shape[0] - span, 2 * LANES), jnp.float32)
    beside, across = core[span:, :].astype(jnp.float32), far[span:, :].astype(jnp.float32)
    above, below = jnp.where(even, across, beside), jnp.where(even, beside, across)
    spread_bands(packed_taps([none, none, above], window, bands.shape[2]), extra, 0)
    spread_bands(packed_taps([below, none, none], window, bands.shape[2]), extra, 1)
    last = rows - 1
    picks = (
        (extra[0], bands[0], bands[1], [turned.at[1], turned.at[0], edge.at[0]]),
        (bands[last - 1], bands[last], extra[1], [edge.at[1], turned.at[last], turned.at[last - 1]]),
    )
    for i, (above, here, below, lines) in enumerate(picks):
        band = adjoint_band(window, above, here, below)

        def write(first, k, value, base=i * cols):
            filt[k, base + first : base + first + BLOCK, :] = value

        adjoint_row(band, lines, cols, write)


def backward_edges(bands, core, far, turned, cols, window):
    _, span, outs = turned.shape
    kernels = bands.shape[1] // BLOCK
    return kernel_call(
        functools.partial(backward_edges_kernel, window, cols),
        [bands, core, far, turned],
        pltpu.VMEM((kernels, 2 * cols, outs), jnp.bfloat16),
        [
            pltpu.VMEM((2, span, outs), jnp.bfloat16),
            pltpu.VMEM((2,) + bands.shape[1:], jnp.bfloat16),
        ],
        8,
    )


def mixed_rows(source, mixing, cols, store):
    total = None
    for k in range(mixing.shape[0]):
        term = lax.dot_general(
            source[k], mixing[k], (((1,), (1,)), ((), ())), preferred_element_type=jnp.float32
        )
        total = term if total is None else total + term
    total = total.astype(jnp.bfloat16)
    back = mirror(cols)
    for i in range(total.shape[0] // cols):
        part = total[i * cols : (i + 1) * cols]
        store(i, jnp.dot(back, part, preferred_element_type=jnp.float32).astype(jnp.bfloat16))


def inner_mix_kernel(mixing, inner, out):
    def store(i, value):
        out[i] = value

    mixed_rows(inner, mixing, out.shape[1], store)


def inner_mix(mixing, inner, cols):
    _, chans, _ = mixing.shape
    shape = (inner.shape[1] // cols, cols, chans)
    return kernel_call(inner_mix_kernel, [mixing, inner], pltpu.VMEM(shape, jnp.bfloat16), [], 8)


def back_mix_kernel(mixing, inner, filt, out, stage, sems):
    rows, cols, _ = out.shape
    copies = [
        pltpu.make_async_copy(inner, out.at[pl.ds(1, rows - 2)], sems.at[0]),
        pltpu.make_async_copy(stage.at[0], out.at[0], sems.at[1]),
        pltpu.make_async_copy(stage.at[1], out.at[rows - 1], sems.at[2]),
    ]
    copies[0].start()

    def store(i, value):
        stage[i] = value

    mixed_rows(filt, mixing, cols, store)
    copies[1].start()
    copies[2].start()
    for copy in copies:
        copy.wait()


def back_mix(mixing, inner, filt, rows):
    _, chans, _ = mixing.shape
    cols = filt.shape[1] // 2
    return kernel_call(
        back_mix_kernel,
        [mixing, inner, filt],
        jax.ShapeDtypeStruct((rows, cols, chans), jnp.bfloat16),
        [pltpu.VMEM((2, cols, chans), jnp.bfloat16), pltpu.SemaphoreType.DMA((3,))],
        8,
        far_out=True,
    )


def assemble_kernel(mine, other, out):
    half, _, piece, _ = mine.shape
    place = band_place(2 * half)
    for m in range(2 * half):
        source = mine[m] if m < half else other[m - half]
        start = pl.multiple_of((place ^ m) * piece, piece)
        out[:, pl.ds(start, piece), :] = source.astype(out.dtype)


def assemble(mine, other):
    half, share, piece, chans = mine.shape
    return kernel_call(
        assemble_kernel,
        [mine, other],
        jax.ShapeDtypeStruct((share, 2 * half * piece, chans), jnp.float32),
        [],
        4,
    )


def reduced_gradient(keep, send):
    n_lat, n_lon = lax.axis_size("lat"), lax.axis_size("lon")
    mask = 1
    while True:
        other = lax.ppermute(send, "lat", swap("lat", mask))
        total = keep + other.astype(jnp.float32)
        mask *= 2
        if mask >= n_lat:
            break
        half = total.shape[0] // 2
        keep, send = total[:half], total[half:].astype(jnp.bfloat16)
    total = total[0]
    wire = total.astype(jnp.bfloat16)
    piece = total[0]
    for s in range(1, n_lon):
        other = lax.ppermute(wire[s], "lon", swap("lon", s))
        piece = piece + other.astype(jnp.float32)
    pieces = piece.astype(jnp.bfloat16)[None]
    while mask > 1:
        mask //= 2
        other = lax.ppermute(pieces, "lat", swap("lat", mask))
        if mask > 1:
            pieces = jnp.concatenate([pieces, other], axis=0)
    return assemble(pieces, other)


def on_device(field_in, quadrature, half_width, mixing, cotangent):
    rows, cols, chans = field_in.shape
    kernels, _, outs = mixing.shape
    taps = quadrature.shape[-1]
    rim = (taps - 1) // 2
    n_lat, n_lon = lax.axis_size("lat"), lax.axis_size("lon")
    groups = split_rows(rows)
    outer = groups[0]

    def beside(pair):
        count = lax.axis_size("lon")
        other = [(i, (i + 1) % count) for i in range(1, count, 2)]
        return [
            lax.ppermute(pair[0], "lon", swap("lon", 1)),
            lax.ppermute(pair[1], "lon", other + [(j, i) for i, j in other]),
        ]

    def bands_beside(pair):
        across = [(i, i + 1) for i in range(1, lax.axis_size("lat") - 1, 2)]
        far = lax.ppermute(pair[1], "lat", across + [(j, i) for i, j in across])
        core = lax.ppermute(pair[0], "lat", swap("lat", 1))
        return core, far

    window = taps - 1 + BLOCK
    sides = rims(field_in, rim, groups)
    outer_sides = beside(sides[0:2])
    inner_sides = beside(sides[2:4])
    *sides, field_near, cot_near, taps_near, reach = loads(
        field_in, cotangent, quadrature, half_width, rim
    )
    g_sides = beside(sides)
    bands, basis_edges = band_matrices(reach, taps_near)
    picks = (0, len(outer) - 1)
    sent = edge_rows(field_near, *outer_sides, picks, [])
    f_core, f_far = bands_beside(sent)

    flat_cot = cot_near.reshape(rows * cols, outs)
    filtered, send = forward(
        bands,
        field_near,
        f_core,
        f_far,
        flat_cot,
        groups,
        outer_sides + inner_sides,
        kernels,
        n_lat,
        n_lon,
    )
    keep = kept(filtered, flat_cot, kernels, n_lat, n_lon)
    weight_grad = reduced_gradient(keep, send)
    field_out = kernel_call(
        mix_kernel,
        [filtered, mixing.reshape(kernels * chans, outs)],
        jax.ShapeDtypeStruct((rows * cols, outs), jnp.bfloat16),
        [],
        8,
    )
    sent = edge_rows(cot_near, *g_sides, (0, rows - 1), [basis_edges])
    g_core, g_far = bands_beside(sent)
    inner, turned = backward_inner(bands, cot_near, *g_sides, window)
    edge = backward_edges(bands, g_core, g_far, turned, cols, window)
    input_grad = back_mix(mixing, inner_mix(mixing, inner, cols), edge, rows)
    return (
        field_out.reshape(rows, cols, outs),
        input_grad,
        weight_grad,
    )


def solution(mesh):
    return jax.shard_map(
        on_device,
        mesh=mesh,
        in_specs=(
            P(("ens", "lat"), "lon", None),
            P("lat", None, None, None),
            P("lat"),
            P(),
            P(("ens", "lat"), "lon", None),
        ),
        out_specs=(
            P(("ens", "lat"), "lon", None),
            P(("ens", "lat"), "lon", None),
            P("lon", "ens", None),
        ),
        check_vma=False,
    )
```

```python
import functools

import jax
import jax.numpy as jnp
from jax import lax
from jax.experimental import pallas as pl
from jax.experimental.pallas import tpu as pltpu
from jax.sharding import PartitionSpec as P


BLOCK = 32
LANES = 128
DEPTH = 256


def swap(axis, mask):
    return [(i, i ^ mask) for i in range(lax.axis_size(axis))]


IN_VMEM = pl.BlockSpec(memory_space=pltpu.VMEM)
IN_SMEM = pl.BlockSpec(memory_space=pltpu.SMEM)
IN_HBM = pl.BlockSpec(memory_space=pltpu.HBM)


def near(array):
    return pltpu.with_memory_space_constraint(array, pltpu.VMEM)


def kernel_call(body, operands, outs, scratch, mib, scalars=0, far=(), far_out=False, alias=None):
    specs = [IN_SMEM] * scalars
    given = [pltpu.with_memory_space_constraint(x, pltpu.HBM) for x in operands[:scalars]]
    for i, operand in enumerate(operands[scalars:], scalars):
        specs.append(IN_HBM if i in far else IN_VMEM)
        given.append(pltpu.with_memory_space_constraint(operand, pltpu.HBM) if i in far else near(operand))
    single = not isinstance(outs, list)
    place = IN_HBM if far_out else IN_VMEM
    return pl.pallas_call(
        body,
        in_specs=specs,
        out_specs=place if single else [place] * len(outs),
        out_shape=outs,
        scratch_shapes=scratch,
        input_output_aliases=alias or {},
        compiler_params=pltpu.CompilerParams(vmem_limit_bytes=mib << 20),
    )(*given)


def packed_taps(pieces, window, total):
    kernels = pieces[0].shape[0]
    packed = None
    for r, piece in enumerate(pieces):
        wide = jnp.concatenate([piece, jnp.zeros((kernels, total - piece.shape[1]), piece.dtype)], 1)
        wide = pltpu.roll(wide, r * window, 1) if r else wide
        packed = wide if packed is None else packed + wide
    return packed


def spread_bands(packed, bands, row):
    kernels, total = packed.shape
    for k in range(kernels):
        rows = jnp.broadcast_to(packed[k : k + 1, :], (BLOCK, total))
        rolled = pltpu.roll(rows, 0, 1, stride=1, stride_axis=0)
        bands[row, k * BLOCK : (k + 1) * BLOCK, :] = rolled.astype(bands.dtype)


def bands_kernel(reach, quadrature, bands, edges):
    rows, three, kernels, taps = quadrature.shape
    window = taps - 1 + BLOCK
    middle = (taps - 1) // 2
    lane = lax.broadcasted_iota(jnp.int32, (kernels, LANES), 1)
    for row in range(rows):
        half = jnp.broadcast_to(reach[row : row + 1, :], (kernels, LANES))
        factor = 1.0 / jnp.sqrt(3.0 * (2.0 * half.astype(jnp.float32) + 1.0))
        head_inside = (jnp.abs(lane - middle) <= half).astype(jnp.float32)
        tail_inside = ((lane < taps - LANES) & (lane + LANES - middle <= half)).astype(jnp.float32)
        pieces = []
        for r in range(three):
            head = quadrature[row, r, :, 0:LANES] * factor * head_inside
            last = jnp.broadcast_to(quadrature[row, r, :, LANES:taps], (kernels, LANES))
            tail = last * factor * tail_inside
            piece = jnp.concatenate([head, tail], axis=1).astype(jnp.bfloat16)
            if row == rows - 1 and r == three - 1:
                edges[0] = piece
            if row == 0 and r == 0:
                edges[1] = piece
            pieces.append(piece.astype(jnp.float32))
        spread_bands(packed_taps(pieces, window, bands.shape[2]), bands, row)


def band_matrices(reach, quadrature):
    rows, three, kernels, taps = quadrature.shape
    total = -(-three * (taps - 1 + BLOCK) // DEPTH) * DEPTH
    return kernel_call(
        bands_kernel,
        [reach, quadrature],
        [
            pltpu.VMEM((rows, kernels * BLOCK, total), jnp.bfloat16),
            pltpu.VMEM((2, kernels, 2 * LANES), jnp.bfloat16),
        ],
        [],
        8,
    )


def split_rows(rows):
    part = 1
    outer = list(range(part)) + list(range(rows - part, rows))
    return outer, list(range(part, rows - part))


def even_sector():
    return lax.rem(lax.axis_index("lon"), 2) == 0


def rim_places(cols, rim):
    even = even_sector()
    first = pl.multiple_of(jnp.where(even, rim + cols, 0), rim)
    second = pl.multiple_of(jnp.where(even, 0, rim + cols), rim)
    return first, second


def rim_copies(groups, array, outs):
    cols = array.shape[1]
    rim = outs[0].shape[1]
    even = even_sector()
    starts = (jnp.where(even, cols - rim, 0), jnp.where(even, 0, cols - rim))
    copies = []
    for g, group in enumerate(groups):
        place = 0
        while place < len(group):
            size = 1
            while place + size < len(group) and group[place + size] == group[place] + size:
                size += 1
            source = array.at[pl.ds(group[place], size)]
            for side, first in enumerate(starts):
                target = outs[2 * g + side].at[pl.ds(place, size)]
                first = pl.multiple_of(first, rim)
                copies.append((source.at[:, pl.ds(first, rim), :], target))
            place += size
    return copies


def rims_kernel(groups, field, *refs):
    *sides, sems = refs
    copies = rim_copies(groups, field, sides)
    copies = [pltpu.make_async_copy(*c, sems.at[i]) for i, c in enumerate(copies)]
    for copy in copies:
        copy.start()
    for copy in copies:
        copy.wait()


def rims(field, rim, groups):
    chans = field.shape[2]
    outs = [
        pltpu.VMEM((len(group), rim, chans), jnp.bfloat16) for group in groups for _ in range(2)
    ]
    return kernel_call(
        functools.partial(rims_kernel, groups),
        [field],
        outs,
        [pltpu.SemaphoreType.DMA((16,))],
        4,
        far=(0,),
    )


def loads_kernel(field, cot, quadrature, half_width, *refs):
    *sides, field_near, cot_near, taps_near, reach, widths, sems = refs
    first = pltpu.make_async_copy(half_width, widths, sems.at[0])
    first.start()
    copies = rim_copies([range(cot.shape[0])], cot, sides)
    copies += [(quadrature, taps_near), (field, field_near), (cot, cot_near)]
    copies = [pltpu.make_async_copy(*c, sems.at[i + 1]) for i, c in enumerate(copies)]
    for copy in copies:
        copy.start()
    first.wait()
    for row in range(reach.shape[0]):
        reach[row : row + 1, :] = jnp.full((1, LANES), widths[row], jnp.int32)
    for copy in copies:
        copy.wait()


def loads(field, cot, quadrature, half_width, rim):
    rows, _, chans = field.shape
    outs = [pltpu.VMEM((rows, rim, chans), jnp.bfloat16)] * 2
    outs.append(pltpu.VMEM(field.shape, field.dtype))
    outs.append(pltpu.VMEM(cot.shape, cot.dtype))
    outs.append(pltpu.VMEM(quadrature.shape, jnp.float32))
    outs.append(pltpu.VMEM((rows, LANES), jnp.int32))
    return kernel_call(
        loads_kernel,
        [field, cot, quadrature, half_width],
        outs,
        [pltpu.SMEM(half_width.shape, jnp.int32), pltpu.SemaphoreType.DMA((8,))],
        8,
        far=(0, 1, 2, 3),
    )


def even_band():
    return lax.rem(lax.axis_index("lat"), 2) == 0


def edges_kernel(picks, own, paired, other, *rest):
    *basis, core_row, far_row = rest
    rim, cols = paired.shape[1], own.shape[1]
    even = even_band()
    first, second = rim_places(cols, rim)
    for out, last in ((core_row, even), (far_row, jnp.logical_not(even))):
        pick = jnp.where(last, picks[1], picks[0])
        out[pl.ds(first, rim)] = paired[pick]
        out[pl.ds(second, rim)] = other[pick]
        out[rim : rim + cols] = own[jnp.where(last, own.shape[0] - 1, 0)]
        if basis:
            out[2 * rim + cols :] = basis[0][jnp.where(last, 0, 1)]


def edge_rows(own, paired, other, picks, basis):
    _, cols, chans = own.shape
    span = cols + 2 * paired.shape[1] + (basis[0].shape[1] if basis else 0)
    outs = [pltpu.VMEM((span, chans), jnp.bfloat16)] * 2
    return kernel_call(
        functools.partial(edges_kernel, picks), [own, paired, other, *basis], outs, [], 4
    )


def fill_extended(ext, own, core, far, groups, sides):
    rows, cols = own.shape[0], own.shape[1]
    rim = sides[0].shape[1]
    span = ext.shape[1]
    even = even_band()
    ext[jnp.where(even, rows + 1, 0)] = core[0:span]
    ext[jnp.where(even, 0, rows + 1)] = far[0:span]
    ext[1 : rows + 1, rim : rim + cols, :] = own[...]
    first, second = rim_places(cols, rim)
    for g, group in enumerate(groups):
        for i, row in enumerate(group):
            ext[row + 1, pl.ds(first, rim), :] = sides[2 * g][i]
            ext[row + 1, pl.ds(second, rim), :] = sides[2 * g + 1][i]


def filter_rows(bands, ext, cols, write):
    rows, height, total = bands.shape
    reach = ext.shape[1] - cols + BLOCK
    spare = total - 3 * reach
    for row in range(rows):
        for first in range(0, cols, BLOCK):
            pieces = [ext[row + r, first : first + reach, :] for r in range(3)]
            if spare:
                pieces.append(ext[row, 0:spare, :])
            source = jnp.concatenate(pieces, axis=0)
            result = jnp.dot(bands[row], source, preferred_element_type=jnp.float32)
            result = result.astype(jnp.bfloat16)
            for k in range(height // BLOCK):
                write(row * cols + first, k, result[k * BLOCK : (k + 1) * BLOCK])


def band_place(n_lat):
    bits = n_lat.bit_length() - 1
    lat = lax.axis_index("lat")
    return sum(((lat >> b) & 1) << (bits - 1 - b) for b in range(bits))


def half_gradient(n_lat, filt, cot, out, grad, slot):
    kernels, half, _ = grad.shape
    n_lon, share, piece = out.shape[1], out.shape[2], out.shape[3]
    place, lon = band_place(n_lat), lax.axis_index("lon")
    group = n_lat // 2
    side = pl.multiple_of(((place // group) ^ slot) * half, half)
    for k in range(kernels):
        grad[k] = lax.dot_general(
            filt[:, pl.ds(side + 2 * half * k, half)],
            cot[...],
            (((0,), (0,)), ((), ())),
            preferred_element_type=jnp.float32,
        )
    for m in range(group):
        start = pl.multiple_of(((place ^ m) % group) * piece, piece)
        for s in range(n_lon):
            first = (lon ^ s) * share
            out[m, s] = grad[pl.ds(first, share), pl.ds(start, piece), :].astype(out.dtype)


def forward_kernel(n_lat, groups, bands, own, core, far, cot, *rest):
    *sides, filt, send, ext, grad = rest
    _, cols, chans = own.shape
    fill_extended(ext, own, core, far, groups, sides)

    def write(start, k, value):
        filt[start : start + BLOCK, k * chans : (k + 1) * chans] = value

    filter_rows(bands, ext, cols, write)
    half_gradient(n_lat, filt, cot, send, grad, 1)


def part_shape(kernels, chans, outs, n_lat, n_lon):
    return (n_lat // 2, n_lon, kernels // n_lon, chans // n_lat, outs)


def forward(bands, own, core, far, cot, groups, sides, kernels, n_lat, n_lon):
    rows, cols, chans = own.shape
    outs = cot.shape[1]
    rim = sides[0].shape[1]
    return kernel_call(
        functools.partial(forward_kernel, n_lat, groups),
        [bands, own, core, far, cot, *sides],
        [
            pltpu.VMEM((rows * cols, kernels * chans), jnp.bfloat16),
            pltpu.VMEM(part_shape(kernels, chans, outs, n_lat, n_lon), jnp.bfloat16),
        ],
        [
            pltpu.VMEM((rows + 2, cols + 2 * rim, chans), jnp.bfloat16),
            pltpu.VMEM((kernels, chans // 2, outs), jnp.float32),
        ],
        20,
    )


def kept_kernel(n_lat, filt, cot, keep, grad):
    half_gradient(n_lat, filt, cot, keep, grad, 0)


def kept(filt, cot, kernels, n_lat, n_lon):
    chans, outs = filt.shape[1] // kernels, cot.shape[1]
    return kernel_call(
        functools.partial(kept_kernel, n_lat),
        [filt, cot],
        pltpu.VMEM(part_shape(kernels, chans, outs, n_lat, n_lon), jnp.float32),
        [pltpu.VMEM((kernels, chans // 2, outs), jnp.float32)],
        12,
    )


def mix_kernel(filt, mixing, out):
    out[...] = jnp.dot(filt[...], mixing[...], preferred_element_type=jnp.float32).astype(out.dtype)


def mirror(size):
    across = lax.broadcasted_iota(jnp.int32, (size, size), 0)
    down = lax.broadcasted_iota(jnp.int32, (size, size), 1)
    return (across + down == size - 1).astype(jnp.float32).astype(jnp.bfloat16)


def adjoint_band(window, above, here, below):
    total = here.shape[1]
    sources = [below, here, above]
    lane = lax.broadcasted_iota(jnp.int32, (here.shape[0], LANES), 1)
    tiles = []
    for first in range(0, total, LANES):
        r = min(first // window, 2)
        tile = sources[r][:, first : first + LANES]
        cut = (r + 1) * window - first
        if r < 2 and cut < LANES:
            following = sources[r + 1][:, first : first + LANES]
            tile = jnp.where(lane < cut, tile, following)
        tiles.append(tile)
    return jnp.concatenate(tiles, axis=1)


def adjoint_row(band, reversed_rows, cols, write):
    span = reversed_rows[0].shape[0]
    reach = span - cols + BLOCK
    spare = band.shape[1] - 3 * reach
    for g in range(cols // BLOCK):
        first = g * BLOCK
        pieces = [source[first : first + reach, :] for source in reversed_rows]
        if spare:
            pieces.append(reversed_rows[0][0:spare, :])
        result = jnp.dot(
            band, jnp.concatenate(pieces, axis=0), preferred_element_type=jnp.float32
        ).astype(jnp.bfloat16)
        for k in range(result.shape[0] // BLOCK):
            write(first, k, result[k * BLOCK : (k + 1) * BLOCK])


def backward_inner_kernel(window, bands, own, paired, other, filt, reverse, lines):
    rows, cols, _ = own.shape
    rim = paired.shape[1]
    flip = mirror(reverse.shape[1])
    first, second = rim_places(cols, rim)
    for row in range(rows):
        lines[row, pl.ds(first, rim), :] = paired[row]
        lines[row, pl.ds(second, rim), :] = other[row]
        lines[row, rim : rim + cols, :] = own[row]
    for row in range(rows):
        reverse[row] = jnp.dot(flip, lines[row], preferred_element_type=jnp.float32).astype(
            reverse.dtype
        )
    for row in range(1, rows - 1):
        band = adjoint_band(window, bands[row - 1], bands[row], bands[row + 1])

        def write(first, k, value, base=(row - 1) * cols):
            filt[k, base + first : base + first + BLOCK, :] = value

        lines = [reverse.at[row + 1], reverse.at[row], reverse.at[row - 1]]
        adjoint_row(band, lines, cols, write)


def backward_inner(bands, own, paired, other, window):
    rows, cols, outs = own.shape
    span = cols + 2 * paired.shape[1]
    kernels = bands.shape[1] // BLOCK
    return kernel_call(
        functools.partial(backward_inner_kernel, window),
        [bands, own, paired, other],
        [
            pltpu.VMEM((kernels, (rows - 2) * cols, outs), jnp.bfloat16),
            pltpu.VMEM((rows, span, outs), jnp.bfloat16),
        ],
        [pltpu.VMEM((rows, span, outs), jnp.bfloat16)],
        12,
    )


def backward_edges_kernel(
    window, cols, bands, core, far, turned, filt, edge, extra
):
    rows, span, _ = turned.shape
    flip = mirror(span)
    even = even_band()
    for i, line in ((jnp.where(even, 1, 0), core), (jnp.where(even, 0, 1), far)):
        edge[i] = jnp.dot(flip, line[0:span], preferred_element_type=jnp.float32).astype(edge.dtype)
    none = jnp.zeros((core.shape[0] - span, 2 * LANES), jnp.float32)
    beside, across = core[span:, :].astype(jnp.float32), far[span:, :].astype(jnp.float32)
    above, below = jnp.where(even, across, beside), jnp.where(even, beside, across)
    spread_bands(packed_taps([none, none, above], window, bands.shape[2]), extra, 0)
    spread_bands(packed_taps([below, none, none], window, bands.shape[2]), extra, 1)
    last = rows - 1
    picks = (
        (extra[0], bands[0], bands[1], [turned.at[1], turned.at[0], edge.at[0]]),
        (bands[last - 1], bands[last], extra[1], [edge.at[1], turned.at[last], turned.at[last - 1]]),
    )
    for i, (above, here, below, lines) in enumerate(picks):
        band = adjoint_band(window, above, here, below)

        def write(first, k, value, base=i * cols):
            filt[k, base + first : base + first + BLOCK, :] = value

        adjoint_row(band, lines, cols, write)


def backward_edges(bands, core, far, turned, cols, window):
    _, span, outs = turned.shape
    kernels = bands.shape[1] // BLOCK
    return kernel_call(
        functools.partial(backward_edges_kernel, window, cols),
        [bands, core, far, turned],
        pltpu.VMEM((kernels, 2 * cols, outs), jnp.bfloat16),
        [
            pltpu.VMEM((2, span, outs), jnp.bfloat16),
            pltpu.VMEM((2,) + bands.shape[1:], jnp.bfloat16),
        ],
        8,
    )


def mixed_rows(source, mixing, first, count, cols, store):
    total = None
    for k in range(mixing.shape[0]):
        term = lax.dot_general(
            source[k, first * cols : (first + count) * cols, :],
            mixing[k],
            (((1,), (1,)), ((), ())),
            preferred_element_type=jnp.float32,
        )
        total = term if total is None else total + term
    total = total.astype(jnp.bfloat16)
    back = mirror(cols)
    for i in range(count):
        part = total[i * cols : (i + 1) * cols]
        store(i, jnp.dot(back, part, preferred_element_type=jnp.float32).astype(jnp.bfloat16))


def inner_mix_kernel(first, mixing, inner, out):
    def store(i, value):
        out[i] = value

    mixed_rows(inner, mixing, first, out.shape[0], out.shape[1], store)


def inner_mix(mixing, inner, first, count, cols):
    shape = (count, cols, mixing.shape[1])
    return kernel_call(
        functools.partial(inner_mix_kernel, first),
        [mixing, inner],
        pltpu.VMEM(shape, jnp.bfloat16),
        [],
        8,
    )


def back_mix_kernel(mixing, upper, lower, filt, out, stage, sems):
    rows, cols, _ = out.shape
    split = 1 + upper.shape[0]
    copies = [
        pltpu.make_async_copy(upper, out.at[pl.ds(1, upper.shape[0])], sems.at[0]),
        pltpu.make_async_copy(lower, out.at[pl.ds(split, lower.shape[0])], sems.at[1]),
        pltpu.make_async_copy(stage.at[0], out.at[0], sems.at[2]),
        pltpu.make_async_copy(stage.at[1], out.at[rows - 1], sems.at[3]),
    ]
    copies[0].start()
    copies[1].start()

    def store(i, value):
        stage[i] = value

    mixed_rows(filt, mixing, 0, 2, cols, store)
    copies[2].start()
    copies[3].start()
    for copy in copies:
        copy.wait()


def back_mix(mixing, upper, lower, filt, rows):
    _, chans, _ = mixing.shape
    cols = filt.shape[1] // 2
    return kernel_call(
        back_mix_kernel,
        [mixing, upper, lower, filt],
        jax.ShapeDtypeStruct((rows, cols, chans), jnp.bfloat16),
        [pltpu.VMEM((2, cols, chans), jnp.bfloat16), pltpu.SemaphoreType.DMA((4,))],
        8,
        far_out=True,
    )


def assemble_kernel(mine, other, out):
    half, _, piece, _ = mine.shape
    place = band_place(2 * half)
    for m in range(2 * half):
        source = mine[m] if m < half else other[m - half]
        start = pl.multiple_of((place ^ m) * piece, piece)
        out[:, pl.ds(start, piece), :] = source.astype(out.dtype)


def assemble(mine, other):
    half, share, piece, chans = mine.shape
    return kernel_call(
        assemble_kernel,
        [mine, other],
        jax.ShapeDtypeStruct((share, 2 * half * piece, chans), jnp.float32),
        [],
        4,
    )


def reduced_gradient(keep, send):
    n_lat, n_lon = lax.axis_size("lat"), lax.axis_size("lon")
    mask = 1
    while True:
        other = lax.ppermute(send, "lat", swap("lat", mask))
        total = keep + other.astype(jnp.float32)
        mask *= 2
        if mask >= n_lat:
            break
        half = total.shape[0] // 2
        keep, send = total[:half], total[half:].astype(jnp.bfloat16)
    total = total[0]
    wire = total.astype(jnp.bfloat16)
    piece = total[0]
    for s in range(1, n_lon):
        other = lax.ppermute(wire[s], "lon", swap("lon", s))
        piece = piece + other.astype(jnp.float32)
    pieces = piece.astype(jnp.bfloat16)[None]
    while mask > 1:
        mask //= 2
        other = lax.ppermute(pieces, "lat", swap("lat", mask))
        if mask > 1:
            pieces = jnp.concatenate([pieces, other], axis=0)
    return assemble(pieces, other)


def on_device(field_in, quadrature, half_width, mixing, cotangent):
    rows, cols, chans = field_in.shape
    kernels, _, outs = mixing.shape
    taps = quadrature.shape[-1]
    rim = (taps - 1) // 2
    n_lat, n_lon = lax.axis_size("lat"), lax.axis_size("lon")
    groups = split_rows(rows)
    outer = groups[0]

    def beside(pair):
        count = lax.axis_size("lon")
        other = [(i, (i + 1) % count) for i in range(1, count, 2)]
        return [
            lax.ppermute(pair[0], "lon", swap("lon", 1)),
            lax.ppermute(pair[1], "lon", other + [(j, i) for i, j in other]),
        ]

    def bands_beside(pair):
        across = [(i, i + 1) for i in range(1, lax.axis_size("lat") - 1, 2)]
        far = lax.ppermute(pair[1], "lat", across + [(j, i) for i, j in across])
        core = lax.ppermute(pair[0], "lat", swap("lat", 1))
        return core, far

    window = taps - 1 + BLOCK
    sides = rims(field_in, rim, groups)
    outer_sides = beside(sides[0:2])
    inner_sides = beside(sides[2:4])
    *sides, field_near, cot_near, taps_near, reach = loads(
        field_in, cotangent, quadrature, half_width, rim
    )
    g_sides = beside(sides)
    bands, basis_edges = band_matrices(reach, taps_near)
    picks = (0, len(outer) - 1)
    sent = edge_rows(field_near, *outer_sides, picks, [])
    f_core, f_far = bands_beside(sent)

    flat_cot = cot_near.reshape(rows * cols, outs)
    filtered, send = forward(
        bands,
        field_near,
        f_core,
        f_far,
        flat_cot,
        groups,
        outer_sides + inner_sides,
        kernels,
        n_lat,
        n_lon,
    )
    keep = kept(filtered, flat_cot, kernels, n_lat, n_lon)
    weight_grad = reduced_gradient(keep, send)
    field_out = kernel_call(
        mix_kernel,
        [filtered, mixing.reshape(kernels * chans, outs)],
        jax.ShapeDtypeStruct((rows * cols, outs), jnp.bfloat16),
        [],
        8,
    )
    sent = edge_rows(cot_near, *g_sides, (0, rows - 1), [basis_edges])
    g_core, g_far = bands_beside(sent)
    inner, turned = backward_inner(bands, cot_near, *g_sides, window)
    edge = backward_edges(bands, g_core, g_far, turned, cols, window)
    half = (rows - 2) // 2
    upper = inner_mix(mixing, inner, 0, half, cols)
    lower = inner_mix(mixing, inner, half, rows - 2 - half, cols)
    input_grad = back_mix(mixing, upper, lower, edge, rows)
    return (
        field_out.reshape(rows, cols, outs),
        input_grad,
        weight_grad,
    )


def solution(mesh):
    return jax.shard_map(
        on_device,
        mesh=mesh,
        in_specs=(
            P(("ens", "lat"), "lon", None),
            P("lat", None, None, None),
            P("lat"),
            P(),
            P(("ens", "lat"), "lon", None),
        ),
        out_specs=(
            P(("ens", "lat"), "lon", None),
            P(("ens", "lat"), "lon", None),
            P("lon", "ens", None),
        ),
        check_vma=False,
    )
```

```python
import functools

import jax
import jax.numpy as jnp
from jax import lax
from jax.experimental import pallas as pl
from jax.experimental.pallas import tpu as pltpu
from jax.sharding import PartitionSpec as P


BLOCK = 32
LANES = 128
DEPTH = 256


def swap(axis, mask):
    return [(i, i ^ mask) for i in range(lax.axis_size(axis))]


IN_VMEM = pl.BlockSpec(memory_space=pltpu.VMEM)
IN_SMEM = pl.BlockSpec(memory_space=pltpu.SMEM)
IN_HBM = pl.BlockSpec(memory_space=pltpu.HBM)


def near(array):
    return pltpu.with_memory_space_constraint(array, pltpu.VMEM)


def kernel_call(body, operands, outs, scratch, mib, scalars=0, far=(), far_out=False, alias=None):
    specs = [IN_SMEM] * scalars
    given = [pltpu.with_memory_space_constraint(x, pltpu.HBM) for x in operands[:scalars]]
    for i, operand in enumerate(operands[scalars:], scalars):
        specs.append(IN_HBM if i in far else IN_VMEM)
        given.append(pltpu.with_memory_space_constraint(operand, pltpu.HBM) if i in far else near(operand))
    single = not isinstance(outs, list)
    place = IN_HBM if far_out else IN_VMEM
    return pl.pallas_call(
        body,
        in_specs=specs,
        out_specs=place if single else [place] * len(outs),
        out_shape=outs,
        scratch_shapes=scratch,
        input_output_aliases=alias or {},
        compiler_params=pltpu.CompilerParams(vmem_limit_bytes=mib << 20),
    )(*given)


def packed_taps(pieces, window, total):
    kernels = pieces[0].shape[0]
    packed = None
    for r, piece in enumerate(pieces):
        wide = jnp.concatenate([piece, jnp.zeros((kernels, total - piece.shape[1]), piece.dtype)], 1)
        wide = pltpu.roll(wide, r * window, 1) if r else wide
        packed = wide if packed is None else packed + wide
    return packed


def spread_bands(packed, bands, row):
    kernels, total = packed.shape
    for k in range(kernels):
        rows = jnp.broadcast_to(packed[k : k + 1, :], (BLOCK, total))
        rolled = pltpu.roll(rows, 0, 1, stride=1, stride_axis=0)
        bands[row, k * BLOCK : (k + 1) * BLOCK, :] = rolled.astype(bands.dtype)


def bands_kernel(reach, quadrature, bands, edges):
    rows, three, kernels, taps = quadrature.shape
    window = taps - 1 + BLOCK
    middle = (taps - 1) // 2
    lane = lax.broadcasted_iota(jnp.int32, (kernels, LANES), 1)
    for row in range(rows):
        half = jnp.broadcast_to(reach[row : row + 1, :], (kernels, LANES))
        factor = 1.0 / jnp.sqrt(3.0 * (2.0 * half.astype(jnp.float32) + 1.0))
        head_inside = (jnp.abs(lane - middle) <= half).astype(jnp.float32)
        tail_inside = ((lane < taps - LANES) & (lane + LANES - middle <= half)).astype(jnp.float32)
        pieces = []
        for r in range(three):
            head = quadrature[row, r, :, 0:LANES] * factor * head_inside
            last = jnp.broadcast_to(quadrature[row, r, :, LANES:taps], (kernels, LANES))
            tail = last * factor * tail_inside
            piece = jnp.concatenate([head, tail], axis=1).astype(jnp.bfloat16)
            if row == rows - 1 and r == three - 1:
                edges[0] = piece
            if row == 0 and r == 0:
                edges[1] = piece
            pieces.append(piece.astype(jnp.float32))
        spread_bands(packed_taps(pieces, window, bands.shape[2]), bands, row)


def band_matrices(reach, quadrature):
    rows, three, kernels, taps = quadrature.shape
    total = -(-three * (taps - 1 + BLOCK) // DEPTH) * DEPTH
    return kernel_call(
        bands_kernel,
        [reach, quadrature],
        [
            pltpu.VMEM((rows, kernels * BLOCK, total), jnp.bfloat16),
            pltpu.VMEM((2, kernels, 2 * LANES), jnp.bfloat16),
        ],
        [],
        8,
    )


def split_rows(rows):
    part = 1
    outer = list(range(part)) + list(range(rows - part, rows))
    return outer, list(range(part, rows - part))


def even_sector():
    return lax.rem(lax.axis_index("lon"), 2) == 0


def rim_places(cols, rim):
    even = even_sector()
    first = pl.multiple_of(jnp.where(even, rim + cols, 0), rim)
    second = pl.multiple_of(jnp.where(even, 0, rim + cols), rim)
    return first, second


def rim_copies(groups, array, outs):
    cols = array.shape[1]
    rim = outs[0].shape[1]
    even = even_sector()
    starts = (jnp.where(even, cols - rim, 0), jnp.where(even, 0, cols - rim))
    copies = []
    for g, group in enumerate(groups):
        place = 0
        while place < len(group):
            size = 1
            while place + size < len(group) and group[place + size] == group[place] + size:
                size += 1
            source = array.at[pl.ds(group[place], size)]
            for side, first in enumerate(starts):
                target = outs[2 * g + side].at[pl.ds(place, size)]
                first = pl.multiple_of(first, rim)
                copies.append((source.at[:, pl.ds(first, rim), :], target))
            place += size
    return copies


def rims_kernel(groups, field, *refs):
    *sides, sems = refs
    copies = rim_copies(groups, field, sides)
    copies = [pltpu.make_async_copy(*c, sems.at[i]) for i, c in enumerate(copies)]
    for copy in copies:
        copy.start()
    for copy in copies:
        copy.wait()


def rims(field, rim, groups):
    chans = field.shape[2]
    outs = [
        pltpu.VMEM((len(group), rim, chans), jnp.bfloat16) for group in groups for _ in range(2)
    ]
    return kernel_call(
        functools.partial(rims_kernel, groups),
        [field],
        outs,
        [pltpu.SemaphoreType.DMA((16,))],
        4,
        far=(0,),
    )


def loads_kernel(field, cot, quadrature, half_width, *refs):
    *sides, field_near, cot_near, taps_near, reach, widths, sems = refs
    first = pltpu.make_async_copy(half_width, widths, sems.at[0])
    first.start()
    copies = rim_copies([range(cot.shape[0])], cot, sides)
    copies += [(quadrature, taps_near), (field, field_near), (cot, cot_near)]
    copies = [pltpu.make_async_copy(*c, sems.at[i + 1]) for i, c in enumerate(copies)]
    for copy in copies:
        copy.start()
    first.wait()
    for row in range(reach.shape[0]):
        reach[row : row + 1, :] = jnp.full((1, LANES), widths[row], jnp.int32)
    for copy in copies:
        copy.wait()


def loads(field, cot, quadrature, half_width, rim):
    rows, _, chans = field.shape
    outs = [pltpu.VMEM((rows, rim, chans), jnp.bfloat16)] * 2
    outs.append(pltpu.VMEM(field.shape, field.dtype))
    outs.append(pltpu.VMEM(cot.shape, cot.dtype))
    outs.append(pltpu.VMEM(quadrature.shape, jnp.float32))
    outs.append(pltpu.VMEM((rows, LANES), jnp.int32))
    return kernel_call(
        loads_kernel,
        [field, cot, quadrature, half_width],
        outs,
        [pltpu.SMEM(half_width.shape, jnp.int32), pltpu.SemaphoreType.DMA((8,))],
        8,
        far=(0, 1, 2, 3),
    )


def even_band():
    return lax.rem(lax.axis_index("lat"), 2) == 0


def edges_kernel(picks, own, paired, other, *rest):
    *basis, core_row, far_row = rest
    rim, cols = paired.shape[1], own.shape[1]
    even = even_band()
    first, second = rim_places(cols, rim)
    for out, last in ((core_row, even), (far_row, jnp.logical_not(even))):
        pick = jnp.where(last, picks[1], picks[0])
        out[pl.ds(first, rim)] = paired[pick]
        out[pl.ds(second, rim)] = other[pick]
        out[rim : rim + cols] = own[jnp.where(last, own.shape[0] - 1, 0)]
        if basis:
            out[2 * rim + cols :] = basis[0][jnp.where(last, 0, 1)]


def edge_rows(own, paired, other, picks, basis):
    _, cols, chans = own.shape
    span = cols + 2 * paired.shape[1] + (basis[0].shape[1] if basis else 0)
    outs = [pltpu.VMEM((span, chans), jnp.bfloat16)] * 2
    return kernel_call(
        functools.partial(edges_kernel, picks), [own, paired, other, *basis], outs, [], 4
    )


def fill_extended(ext, own, core, far, groups, sides):
    rows, cols = own.shape[0], own.shape[1]
    rim = sides[0].shape[1]
    span = ext.shape[1]
    even = even_band()
    ext[jnp.where(even, rows + 1, 0)] = core[0:span]
    ext[jnp.where(even, 0, rows + 1)] = far[0:span]
    ext[1 : rows + 1, rim : rim + cols, :] = own[...]
    first, second = rim_places(cols, rim)
    for g, group in enumerate(groups):
        for i, row in enumerate(group):
            ext[row + 1, pl.ds(first, rim), :] = sides[2 * g][i]
            ext[row + 1, pl.ds(second, rim), :] = sides[2 * g + 1][i]


def filter_rows(bands, ext, cols, write):
    rows, height, total = bands.shape
    reach = ext.shape[1] - cols + BLOCK
    spare = total - 3 * reach
    for row in range(rows):
        for first in range(0, cols, BLOCK):
            pieces = [ext[row + r, first : first + reach, :] for r in range(3)]
            if spare:
                pieces.append(ext[row, 0:spare, :])
            source = jnp.concatenate(pieces, axis=0)
            result = jnp.dot(bands[row], source, preferred_element_type=jnp.float32)
            result = result.astype(jnp.bfloat16)
            for k in range(height // BLOCK):
                write(row * cols + first, k, result[k * BLOCK : (k + 1) * BLOCK])


def band_place(n_lat):
    bits = n_lat.bit_length() - 1
    lat = lax.axis_index("lat")
    return sum(((lat >> b) & 1) << (bits - 1 - b) for b in range(bits))


def half_gradient(n_lat, filt, cot, outs_of, grad, slot):
    kernels, half, _ = grad.shape
    n_lon, share, piece = outs_of[0].shape[1:4]
    place, lon = band_place(n_lat), lax.axis_index("lon")
    group = n_lat // 2
    side = pl.multiple_of(((place // group) ^ slot) * half, half)
    for k in range(kernels):
        grad[k] = lax.dot_general(
            filt[:, pl.ds(side + 2 * half * k, half)],
            cot[...],
            (((0,), (0,)), ((), ())),
            preferred_element_type=jnp.float32,
        )
    for m in range(group):
        start = pl.multiple_of(((place ^ m) % group) * piece, piece)
        out, slot_of = outs_of[2 * m // group], m % (group // 2)
        for s in range(n_lon):
            first = (lon ^ s) * share
            value = grad[pl.ds(first, share), pl.ds(start, piece), :]
            out[slot_of, s] = value.astype(out.dtype)


def forward_kernel(n_lat, groups, bands, own, core, far, cot, *rest):
    *sides, filt, send_low, send_high, ext, grad = rest
    _, cols, chans = own.shape
    fill_extended(ext, own, core, far, groups, sides)

    def write(start, k, value):
        filt[start : start + BLOCK, k * chans : (k + 1) * chans] = value

    filter_rows(bands, ext, cols, write)
    half_gradient(n_lat, filt, cot, (send_low, send_high), grad, 1)


def part_shape(kernels, chans, outs, n_lat, n_lon):
    return (n_lat // 4, n_lon, kernels // n_lon, chans // n_lat, outs)


def forward(bands, own, core, far, cot, groups, sides, kernels, n_lat, n_lon):
    rows, cols, chans = own.shape
    outs = cot.shape[1]
    rim = sides[0].shape[1]
    return kernel_call(
        functools.partial(forward_kernel, n_lat, groups),
        [bands, own, core, far, cot, *sides],
        [
            pltpu.VMEM((rows * cols, kernels * chans), jnp.bfloat16),
            pltpu.VMEM(part_shape(kernels, chans, outs, n_lat, n_lon), jnp.bfloat16),
            pltpu.VMEM(part_shape(kernels, chans, outs, n_lat, n_lon), jnp.bfloat16),
        ],
        [
            pltpu.VMEM((rows + 2, cols + 2 * rim, chans), jnp.bfloat16),
            pltpu.VMEM((kernels, chans // 2, outs), jnp.float32),
        ],
        20,
    )


def kept_kernel(n_lat, filt, cot, keep_low, keep_high, grad):
    half_gradient(n_lat, filt, cot, (keep_low, keep_high), grad, 0)


def kept(filt, cot, kernels, n_lat, n_lon):
    chans, outs = filt.shape[1] // kernels, cot.shape[1]
    return kernel_call(
        functools.partial(kept_kernel, n_lat),
        [filt, cot],
        [pltpu.VMEM(part_shape(kernels, chans, outs, n_lat, n_lon), jnp.float32)] * 2,
        [pltpu.VMEM((kernels, chans // 2, outs), jnp.float32)],
        12,
    )


def mix_kernel(filt, mixing, out):
    out[...] = jnp.dot(filt[...], mixing[...], preferred_element_type=jnp.float32).astype(out.dtype)


def mirror(size):
    across = lax.broadcasted_iota(jnp.int32, (size, size), 0)
    down = lax.broadcasted_iota(jnp.int32, (size, size), 1)
    return (across + down == size - 1).astype(jnp.float32).astype(jnp.bfloat16)


def adjoint_band(window, above, here, below):
    total = here.shape[1]
    sources = [below, here, above]
    lane = lax.broadcasted_iota(jnp.int32, (here.shape[0], LANES), 1)
    tiles = []
    for first in range(0, total, LANES):
        r = min(first // window, 2)
        tile = sources[r][:, first : first + LANES]
        cut = (r + 1) * window - first
        if r < 2 and cut < LANES:
            following = sources[r + 1][:, first : first + LANES]
            tile = jnp.where(lane < cut, tile, following)
        tiles.append(tile)
    return jnp.concatenate(tiles, axis=1)


def adjoint_row(band, reversed_rows, cols, write):
    span = reversed_rows[0].shape[0]
    reach = span - cols + BLOCK
    spare = band.shape[1] - 3 * reach
    for g in range(cols // BLOCK):
        first = g * BLOCK
        pieces = [source[first : first + reach, :] for source in reversed_rows]
        if spare:
            pieces.append(reversed_rows[0][0:spare, :])
        result = jnp.dot(
            band, jnp.concatenate(pieces, axis=0), preferred_element_type=jnp.float32
        ).astype(jnp.bfloat16)
        for k in range(result.shape[0] // BLOCK):
            write(first, k, result[k * BLOCK : (k + 1) * BLOCK])


def backward_inner_kernel(window, bands, own, paired, other, filt, reverse, lines):
    rows, cols, _ = own.shape
    rim = paired.shape[1]
    flip = mirror(reverse.shape[1])
    first, second = rim_places(cols, rim)
    for row in range(rows):
        lines[row, pl.ds(first, rim), :] = paired[row]
        lines[row, pl.ds(second, rim), :] = other[row]
        lines[row, rim : rim + cols, :] = own[row]
    for row in range(rows):
        reverse[row] = jnp.dot(flip, lines[row], preferred_element_type=jnp.float32).astype(
            reverse.dtype
        )
    for row in range(1, rows - 1):
        band = adjoint_band(window, bands[row - 1], bands[row], bands[row + 1])

        def write(first, k, value, base=(row - 1) * cols):
            filt[k, base + first : base + first + BLOCK, :] = value

        lines = [reverse.at[row + 1], reverse.at[row], reverse.at[row - 1]]
        adjoint_row(band, lines, cols, write)


def backward_inner(bands, own, paired, other, window):
    rows, cols, outs = own.shape
    span = cols + 2 * paired.shape[1]
    kernels = bands.shape[1] // BLOCK
    return kernel_call(
        functools.partial(backward_inner_kernel, window),
        [bands, own, paired, other],
        [
            pltpu.VMEM((kernels, (rows - 2) * cols, outs), jnp.bfloat16),
            pltpu.VMEM((rows, span, outs), jnp.bfloat16),
        ],
        [pltpu.VMEM((rows, span, outs), jnp.bfloat16)],
        12,
    )


def backward_edges_kernel(
    window, cols, bands, core, far, turned, filt, edge, extra
):
    rows, span, _ = turned.shape
    flip = mirror(span)
    even = even_band()
    for i, line in ((jnp.where(even, 1, 0), core), (jnp.where(even, 0, 1), far)):
        edge[i] = jnp.dot(flip, line[0:span], preferred_element_type=jnp.float32).astype(edge.dtype)
    none = jnp.zeros((core.shape[0] - span, 2 * LANES), jnp.float32)
    beside, across = core[span:, :].astype(jnp.float32), far[span:, :].astype(jnp.float32)
    above, below = jnp.where(even, across, beside), jnp.where(even, beside, across)
    spread_bands(packed_taps([none, none, above], window, bands.shape[2]), extra, 0)
    spread_bands(packed_taps([below, none, none], window, bands.shape[2]), extra, 1)
    last = rows - 1
    picks = (
        (extra[0], bands[0], bands[1], [turned.at[1], turned.at[0], edge.at[0]]),
        (bands[last - 1], bands[last], extra[1], [edge.at[1], turned.at[last], turned.at[last - 1]]),
    )
    for i, (above, here, below, lines) in enumerate(picks):
        band = adjoint_band(window, above, here, below)

        def write(first, k, value, base=i * cols):
            filt[k, base + first : base + first + BLOCK, :] = value

        adjoint_row(band, lines, cols, write)


def backward_edges(bands, core, far, turned, cols, window):
    _, span, outs = turned.shape
    kernels = bands.shape[1] // BLOCK
    return kernel_call(
        functools.partial(backward_edges_kernel, window, cols),
        [bands, core, far, turned],
        pltpu.VMEM((kernels, 2 * cols, outs), jnp.bfloat16),
        [
            pltpu.VMEM((2, span, outs), jnp.bfloat16),
            pltpu.VMEM((2,) + bands.shape[1:], jnp.bfloat16),
        ],
        8,
    )


def mixed_rows(source, mixing, first, count, cols, store):
    total = None
    for k in range(mixing.shape[0]):
        term = lax.dot_general(
            source[k, first * cols : (first + count) * cols, :],
            mixing[k],
            (((1,), (1,)), ((), ())),
            preferred_element_type=jnp.float32,
        )
        total = term if total is None else total + term
    total = total.astype(jnp.bfloat16)
    back = mirror(cols)
    for i in range(count):
        part = total[i * cols : (i + 1) * cols]
        store(i, jnp.dot(back, part, preferred_element_type=jnp.float32).astype(jnp.bfloat16))


def inner_mix_kernel(first, mixing, inner, out):
    def store(i, value):
        out[i] = value

    mixed_rows(inner, mixing, first, out.shape[0], out.shape[1], store)


def inner_mix(mixing, inner, first, count, cols):
    shape = (count, cols, mixing.shape[1])
    return kernel_call(
        functools.partial(inner_mix_kernel, first),
        [mixing, inner],
        pltpu.VMEM(shape, jnp.bfloat16),
        [],
        8,
    )


def back_mix_kernel(mixing, upper, lower, filt, out, stage, sems):
    rows, cols, _ = out.shape
    split = 1 + upper.shape[0]
    copies = [
        pltpu.make_async_copy(upper, out.at[pl.ds(1, upper.shape[0])], sems.at[0]),
        pltpu.make_async_copy(lower, out.at[pl.ds(split, lower.shape[0])], sems.at[1]),
        pltpu.make_async_copy(stage.at[0], out.at[0], sems.at[2]),
        pltpu.make_async_copy(stage.at[1], out.at[rows - 1], sems.at[3]),
    ]
    copies[0].start()
    copies[1].start()

    def store(i, value):
        stage[i] = value

    mixed_rows(filt, mixing, 0, 2, cols, store)
    copies[2].start()
    copies[3].start()
    for copy in copies:
        copy.wait()


def back_mix(mixing, upper, lower, filt, rows):
    _, chans, _ = mixing.shape
    cols = filt.shape[1] // 2
    return kernel_call(
        back_mix_kernel,
        [mixing, upper, lower, filt],
        jax.ShapeDtypeStruct((rows, cols, chans), jnp.bfloat16),
        [pltpu.VMEM((2, cols, chans), jnp.bfloat16), pltpu.SemaphoreType.DMA((4,))],
        8,
        far_out=True,
    )


def assemble_kernel(mine, other, out):
    half, _, piece, _ = mine.shape
    place = band_place(2 * half)
    for m in range(2 * half):
        source = mine[m] if m < half else other[m - half]
        start = pl.multiple_of((place ^ m) * piece, piece)
        out[:, pl.ds(start, piece), :] = source.astype(out.dtype)


def assemble(mine, other):
    half, share, piece, chans = mine.shape
    return kernel_call(
        assemble_kernel,
        [mine, other],
        jax.ShapeDtypeStruct((share, 2 * half * piece, chans), jnp.float32),
        [],
        4,
    )


def reduced_gradient(keep, send):
    n_lat, n_lon = lax.axis_size("lat"), lax.axis_size("lon")
    high = lax.ppermute(send[1], "lat", swap("lat", 1))
    low = lax.ppermute(send[0], "lat", swap("lat", 1))
    send = (keep[1] + high.astype(jnp.float32)).astype(jnp.bfloat16)
    keep = keep[0] + low.astype(jnp.float32)
    mask = 2
    while True:
        other = lax.ppermute(send, "lat", swap("lat", mask))
        total = keep + other.astype(jnp.float32)
        mask *= 2
        if mask >= n_lat:
            break
        half = total.shape[0] // 2
        keep, send = total[:half], total[half:].astype(jnp.bfloat16)
    total = total[0]
    wire = total.astype(jnp.bfloat16)
    piece = total[0]
    for s in range(1, n_lon):
        other = lax.ppermute(wire[s], "lon", swap("lon", s))
        piece = piece + other.astype(jnp.float32)
    pieces = piece.astype(jnp.bfloat16)[None]
    while mask > 1:
        mask //= 2
        other = lax.ppermute(pieces, "lat", swap("lat", mask))
        if mask > 1:
            pieces = jnp.concatenate([pieces, other], axis=0)
    return assemble(pieces, other)


def on_device(field_in, quadrature, half_width, mixing, cotangent):
    rows, cols, chans = field_in.shape
    kernels, _, outs = mixing.shape
    taps = quadrature.shape[-1]
    rim = (taps - 1) // 2
    n_lat, n_lon = lax.axis_size("lat"), lax.axis_size("lon")
    groups = split_rows(rows)
    outer = groups[0]

    def beside(pair):
        count = lax.axis_size("lon")
        other = [(i, (i + 1) % count) for i in range(1, count, 2)]
        return [
            lax.ppermute(pair[0], "lon", swap("lon", 1)),
            lax.ppermute(pair[1], "lon", other + [(j, i) for i, j in other]),
        ]

    def bands_beside(pair):
        across = [(i, i + 1) for i in range(1, lax.axis_size("lat") - 1, 2)]
        far = lax.ppermute(pair[1], "lat", across + [(j, i) for i, j in across])
        core = lax.ppermute(pair[0], "lat", swap("lat", 1))
        return core, far

    window = taps - 1 + BLOCK
    sides = rims(field_in, rim, groups)
    outer_sides = beside(sides[0:2])
    inner_sides = beside(sides[2:4])
    *sides, field_near, cot_near, taps_near, reach = loads(
        field_in, cotangent, quadrature, half_width, rim
    )
    g_sides = beside(sides)
    bands, basis_edges = band_matrices(reach, taps_near)
    picks = (0, len(outer) - 1)
    sent = edge_rows(field_near, *outer_sides, picks, [])
    f_core, f_far = bands_beside(sent)

    flat_cot = cot_near.reshape(rows * cols, outs)
    filtered, *send = forward(
        bands,
        field_near,
        f_core,
        f_far,
        flat_cot,
        groups,
        outer_sides + inner_sides,
        kernels,
        n_lat,
        n_lon,
    )
    keep = kept(filtered, flat_cot, kernels, n_lat, n_lon)
    weight_grad = reduced_gradient(keep, send)
    field_out = kernel_call(
        mix_kernel,
        [filtered, mixing.reshape(kernels * chans, outs)],
        jax.ShapeDtypeStruct((rows * cols, outs), jnp.bfloat16),
        [],
        8,
    )
    sent = edge_rows(cot_near, *g_sides, (0, rows - 1), [basis_edges])
    g_core, g_far = bands_beside(sent)
    inner, turned = backward_inner(bands, cot_near, *g_sides, window)
    edge = backward_edges(bands, g_core, g_far, turned, cols, window)
    half = (rows - 2) // 2
    upper = inner_mix(mixing, inner, 0, half, cols)
    lower = inner_mix(mixing, inner, half, rows - 2 - half, cols)
    input_grad = back_mix(mixing, upper, lower, edge, rows)
    return (
        field_out.reshape(rows, cols, outs),
        input_grad,
        weight_grad,
    )


def solution(mesh):
    return jax.shard_map(
        on_device,
        mesh=mesh,
        in_specs=(
            P(("ens", "lat"), "lon", None),
            P("lat", None, None, None),
            P("lat"),
            P(),
            P(("ens", "lat"), "lon", None),
        ),
        out_specs=(
            P(("ens", "lat"), "lon", None),
            P(("ens", "lat"), "lon", None),
            P("lon", "ens", None),
        ),
        check_vma=False,
    )
```

```python
import functools

import jax
import jax.numpy as jnp
from jax import lax
from jax.experimental import pallas as pl
from jax.experimental.pallas import tpu as pltpu
from jax.sharding import PartitionSpec as P


BLOCK = 32
LANES = 128
DEPTH = 256


def swap(axis, mask):
    return [(i, i ^ mask) for i in range(lax.axis_size(axis))]


IN_VMEM = pl.BlockSpec(memory_space=pltpu.VMEM)
IN_SMEM = pl.BlockSpec(memory_space=pltpu.SMEM)
IN_HBM = pl.BlockSpec(memory_space=pltpu.HBM)


def near(array):
    return pltpu.with_memory_space_constraint(array, pltpu.VMEM)


def kernel_call(body, operands, outs, scratch, mib, scalars=0, far=(), far_out=False, alias=None):
    specs = [IN_SMEM] * scalars
    given = [pltpu.with_memory_space_constraint(x, pltpu.HBM) for x in operands[:scalars]]
    for i, operand in enumerate(operands[scalars:], scalars):
        specs.append(IN_HBM if i in far else IN_VMEM)
        given.append(pltpu.with_memory_space_constraint(operand, pltpu.HBM) if i in far else near(operand))
    single = not isinstance(outs, list)
    place = IN_HBM if far_out else IN_VMEM
    return pl.pallas_call(
        body,
        in_specs=specs,
        out_specs=place if single else [place] * len(outs),
        out_shape=outs,
        scratch_shapes=scratch,
        input_output_aliases=alias or {},
        compiler_params=pltpu.CompilerParams(vmem_limit_bytes=mib << 20),
    )(*given)


def packed_taps(pieces, window, total):
    kernels = pieces[0].shape[0]
    packed = None
    for r, piece in enumerate(pieces):
        wide = jnp.concatenate([piece, jnp.zeros((kernels, total - piece.shape[1]), piece.dtype)], 1)
        wide = pltpu.roll(wide, r * window, 1) if r else wide
        packed = wide if packed is None else packed + wide
    return packed


def spread_bands(packed, bands, row):
    kernels, total = packed.shape
    for k in range(kernels):
        rows = jnp.broadcast_to(packed[k : k + 1, :], (BLOCK, total))
        rolled = pltpu.roll(rows, 0, 1, stride=1, stride_axis=0)
        bands[row, k * BLOCK : (k + 1) * BLOCK, :] = rolled.astype(bands.dtype)


def bands_kernel(reach, quadrature, bands, edges):
    rows, three, kernels, taps = quadrature.shape
    window = taps - 1 + BLOCK
    middle = (taps - 1) // 2
    lane = lax.broadcasted_iota(jnp.int32, (kernels, LANES), 1)
    for row in range(rows):
        half = jnp.broadcast_to(reach[row : row + 1, :], (kernels, LANES))
        factor = 1.0 / jnp.sqrt(3.0 * (2.0 * half.astype(jnp.float32) + 1.0))
        head_inside = (jnp.abs(lane - middle) <= half).astype(jnp.float32)
        tail_inside = ((lane < taps - LANES) & (lane + LANES - middle <= half)).astype(jnp.float32)
        pieces = []
        for r in range(three):
            head = quadrature[row, r, :, 0:LANES] * factor * head_inside
            last = jnp.broadcast_to(quadrature[row, r, :, LANES:taps], (kernels, LANES))
            tail = last * factor * tail_inside
            piece = jnp.concatenate([head, tail], axis=1).astype(jnp.bfloat16)
            if row == rows - 1 and r == three - 1:
                edges[0] = piece
            if row == 0 and r == 0:
                edges[1] = piece
            pieces.append(piece.astype(jnp.float32))
        spread_bands(packed_taps(pieces, window, bands.shape[2]), bands, row)


def band_matrices(reach, quadrature):
    rows, three, kernels, taps = quadrature.shape
    total = -(-three * (taps - 1 + BLOCK) // DEPTH) * DEPTH
    return kernel_call(
        bands_kernel,
        [reach, quadrature],
        [
            pltpu.VMEM((rows, kernels * BLOCK, total), jnp.bfloat16),
            pltpu.VMEM((2, kernels, 2 * LANES), jnp.bfloat16),
        ],
        [],
        8,
    )


def split_rows(rows):
    part = 1
    outer = list(range(part)) + list(range(rows - part, rows))
    return outer, list(range(part, rows - part))


def even_sector():
    return lax.rem(lax.axis_index("lon"), 2) == 0


def rim_places(cols, rim):
    even = even_sector()
    first = pl.multiple_of(jnp.where(even, rim + cols, 0), rim)
    second = pl.multiple_of(jnp.where(even, 0, rim + cols), rim)
    return first, second


def rim_copies(groups, array, outs):
    cols = array.shape[1]
    rim = outs[0].shape[1]
    even = even_sector()
    starts = (jnp.where(even, cols - rim, 0), jnp.where(even, 0, cols - rim))
    copies = []
    for g, group in enumerate(groups):
        place = 0
        while place < len(group):
            size = 1
            while place + size < len(group) and group[place + size] == group[place] + size:
                size += 1
            source = array.at[pl.ds(group[place], size)]
            for side, first in enumerate(starts):
                target = outs[2 * g + side].at[pl.ds(place, size)]
                first = pl.multiple_of(first, rim)
                copies.append((source.at[:, pl.ds(first, rim), :], target))
            place += size
    return copies


def rims_kernel(groups, field, *refs):
    *sides, sems = refs
    copies = rim_copies(groups, field, sides)
    copies = [pltpu.make_async_copy(*c, sems.at[i]) for i, c in enumerate(copies)]
    for copy in copies:
        copy.start()
    for copy in copies:
        copy.wait()


def rims(field, rim, groups):
    chans = field.shape[2]
    outs = [
        pltpu.VMEM((len(group), rim, chans), jnp.bfloat16) for group in groups for _ in range(2)
    ]
    return kernel_call(
        functools.partial(rims_kernel, groups),
        [field],
        outs,
        [pltpu.SemaphoreType.DMA((16,))],
        4,
        far=(0,),
    )


def loads_kernel(field, cot, quadrature, half_width, *refs):
    *sides, field_near, cot_near, taps_near, reach, widths, sems = refs
    first = pltpu.make_async_copy(half_width, widths, sems.at[0])
    first.start()
    copies = rim_copies([range(cot.shape[0])], cot, sides)
    copies += [(quadrature, taps_near), (field, field_near), (cot, cot_near)]
    copies = [pltpu.make_async_copy(*c, sems.at[i + 1]) for i, c in enumerate(copies)]
    for copy in copies:
        copy.start()
    first.wait()
    for row in range(reach.shape[0]):
        reach[row : row + 1, :] = jnp.full((1, LANES), widths[row], jnp.int32)
    for copy in copies:
        copy.wait()


def loads(field, cot, quadrature, half_width, rim):
    rows, _, chans = field.shape
    outs = [pltpu.VMEM((rows, rim, chans), jnp.bfloat16)] * 2
    outs.append(pltpu.VMEM(field.shape, field.dtype))
    outs.append(pltpu.VMEM(cot.shape, cot.dtype))
    outs.append(pltpu.VMEM(quadrature.shape, jnp.float32))
    outs.append(pltpu.VMEM((rows, LANES), jnp.int32))
    return kernel_call(
        loads_kernel,
        [field, cot, quadrature, half_width],
        outs,
        [pltpu.SMEM(half_width.shape, jnp.int32), pltpu.SemaphoreType.DMA((8,))],
        8,
        far=(0, 1, 2, 3),
    )


def even_band():
    return lax.rem(lax.axis_index("lat"), 2) == 0


def edges_kernel(picks, own, paired, other, *rest):
    *basis, core_row, far_row = rest
    rim, cols = paired.shape[1], own.shape[1]
    even = even_band()
    first, second = rim_places(cols, rim)
    for out, last in ((core_row, even), (far_row, jnp.logical_not(even))):
        pick = jnp.where(last, picks[1], picks[0])
        out[pl.ds(first, rim)] = paired[pick]
        out[pl.ds(second, rim)] = other[pick]
        out[rim : rim + cols] = own[jnp.where(last, own.shape[0] - 1, 0)]
        if basis:
            out[2 * rim + cols :] = basis[0][jnp.where(last, 0, 1)]


def edge_rows(own, paired, other, picks, basis):
    _, cols, chans = own.shape
    span = cols + 2 * paired.shape[1] + (basis[0].shape[1] if basis else 0)
    outs = [pltpu.VMEM((span, chans), jnp.bfloat16)] * 2
    return kernel_call(
        functools.partial(edges_kernel, picks), [own, paired, other, *basis], outs, [], 4
    )


def fill_extended(ext, own, core, far, groups, sides):
    rows, cols = own.shape[0], own.shape[1]
    rim = sides[0].shape[1]
    span = ext.shape[1]
    even = even_band()
    ext[jnp.where(even, rows + 1, 0)] = core[0:span]
    ext[jnp.where(even, 0, rows + 1)] = far[0:span]
    ext[1 : rows + 1, rim : rim + cols, :] = own[...]
    first, second = rim_places(cols, rim)
    for g, group in enumerate(groups):
        for i, row in enumerate(group):
            ext[row + 1, pl.ds(first, rim), :] = sides[2 * g][i]
            ext[row + 1, pl.ds(second, rim), :] = sides[2 * g + 1][i]


def filter_rows(bands, ext, cols, write):
    rows, height, total = bands.shape
    reach = ext.shape[1] - cols + BLOCK
    spare = total - 3 * reach
    for row in range(rows):
        for first in range(0, cols, BLOCK):
            pieces = [ext[row + r, first : first + reach, :] for r in range(3)]
            if spare:
                pieces.append(ext[row, 0:spare, :])
            source = jnp.concatenate(pieces, axis=0)
            result = jnp.dot(bands[row], source, preferred_element_type=jnp.float32)
            result = result.astype(jnp.bfloat16)
            for k in range(height // BLOCK):
                write(row * cols + first, k, result[k * BLOCK : (k + 1) * BLOCK])


def band_place(n_lat):
    bits = n_lat.bit_length() - 1
    lat = lax.axis_index("lat")
    return sum(((lat >> b) & 1) << (bits - 1 - b) for b in range(bits))


def half_gradient(n_lat, filt, cot, outs_of, grad, slot):
    kernels, half, _ = grad.shape
    n_lon, share, piece = outs_of[0].shape[1:4]
    place, lon = band_place(n_lat), lax.axis_index("lon")
    group = n_lat // 2
    side = pl.multiple_of(((place // group) ^ slot) * half, half)
    for k in range(kernels):
        grad[k] = lax.dot_general(
            filt[:, pl.ds(side + 2 * half * k, half)],
            cot[...],
            (((0,), (0,)), ((), ())),
            preferred_element_type=jnp.float32,
        )
    for m in range(group):
        start = pl.multiple_of(((place ^ m) % group) * piece, piece)
        out, slot_of = outs_of[2 * m // group], m % (group // 2)
        for s in range(n_lon):
            first = (lon ^ s) * share
            value = grad[pl.ds(first, share), pl.ds(start, piece), :]
            out[slot_of, s] = value.astype(out.dtype)


def forward_kernel(n_lat, groups, bands, own, core, far, cot, *rest):
    *sides, filt, send_low, send_high, ext, grad = rest
    _, cols, chans = own.shape
    fill_extended(ext, own, core, far, groups, sides)

    def write(start, k, value):
        filt[start : start + BLOCK, k * chans : (k + 1) * chans] = value

    filter_rows(bands, ext, cols, write)
    half_gradient(n_lat, filt, cot, (send_low, send_high), grad, 1)


def part_shape(kernels, chans, outs, n_lat, n_lon):
    return (n_lat // 4, n_lon, kernels // n_lon, chans // n_lat, outs)


def forward(bands, own, core, far, cot, groups, sides, kernels, n_lat, n_lon):
    rows, cols, chans = own.shape
    outs = cot.shape[1]
    rim = sides[0].shape[1]
    return kernel_call(
        functools.partial(forward_kernel, n_lat, groups),
        [bands, own, core, far, cot, *sides],
        [
            pltpu.VMEM((rows * cols, kernels * chans), jnp.bfloat16),
            pltpu.VMEM(part_shape(kernels, chans, outs, n_lat, n_lon), jnp.bfloat16),
            pltpu.VMEM(part_shape(kernels, chans, outs, n_lat, n_lon), jnp.bfloat16),
        ],
        [
            pltpu.VMEM((rows + 2, cols + 2 * rim, chans), jnp.bfloat16),
            pltpu.VMEM((kernels, chans // 2, outs), jnp.float32),
        ],
        20,
    )


def kept_kernel(n_lat, filt, cot, keep_low, keep_high, grad):
    half_gradient(n_lat, filt, cot, (keep_low, keep_high), grad, 0)


def kept(filt, cot, kernels, n_lat, n_lon):
    chans, outs = filt.shape[1] // kernels, cot.shape[1]
    return kernel_call(
        functools.partial(kept_kernel, n_lat),
        [filt, cot],
        [pltpu.VMEM(part_shape(kernels, chans, outs, n_lat, n_lon), jnp.float32)] * 2,
        [pltpu.VMEM((kernels, chans // 2, outs), jnp.float32)],
        12,
    )


def mix_kernel(filt, mixing, out):
    out[...] = jnp.dot(filt[...], mixing[...], preferred_element_type=jnp.float32).astype(out.dtype)


def mirror(size):
    across = lax.broadcasted_iota(jnp.int32, (size, size), 0)
    down = lax.broadcasted_iota(jnp.int32, (size, size), 1)
    return (across + down == size - 1).astype(jnp.float32).astype(jnp.bfloat16)


def adjoint_band(window, above, here, below):
    total = here.shape[1]
    sources = [below, here, above]
    lane = lax.broadcasted_iota(jnp.int32, (here.shape[0], LANES), 1)
    tiles = []
    for first in range(0, total, LANES):
        r = min(first // window, 2)
        tile = sources[r][:, first : first + LANES]
        cut = (r + 1) * window - first
        if r < 2 and cut < LANES:
            following = sources[r + 1][:, first : first + LANES]
            tile = jnp.where(lane < cut, tile, following)
        tiles.append(tile)
    return jnp.concatenate(tiles, axis=1)


def adjoint_row(band, reversed_rows, cols, write):
    span = reversed_rows[0].shape[0]
    reach = span - cols + BLOCK
    spare = band.shape[1] - 3 * reach
    for g in range(cols // BLOCK):
        first = g * BLOCK
        pieces = [source[first : first + reach, :] for source in reversed_rows]
        if spare:
            pieces.append(reversed_rows[0][0:spare, :])
        result = jnp.dot(
            band, jnp.concatenate(pieces, axis=0), preferred_element_type=jnp.float32
        ).astype(jnp.bfloat16)
        for k in range(result.shape[0] // BLOCK):
            write(first, k, result[k * BLOCK : (k + 1) * BLOCK])


def backward_inner_kernel(window, bands, own, paired, other, filt, reverse, lines):
    rows, cols, _ = own.shape
    rim = paired.shape[1]
    flip = mirror(reverse.shape[1])
    first, second = rim_places(cols, rim)
    for row in range(rows):
        lines[row, pl.ds(first, rim), :] = paired[row]
        lines[row, pl.ds(second, rim), :] = other[row]
        lines[row, rim : rim + cols, :] = own[row]
    for row in range(rows):
        reverse[row] = jnp.dot(flip, lines[row], preferred_element_type=jnp.float32).astype(
            reverse.dtype
        )
    for row in range(1, rows - 1):
        band = adjoint_band(window, bands[row - 1], bands[row], bands[row + 1])

        def write(first, k, value, base=(row - 1) * cols):
            filt[k, base + first : base + first + BLOCK, :] = value

        lines = [reverse.at[row + 1], reverse.at[row], reverse.at[row - 1]]
        adjoint_row(band, lines, cols, write)


def backward_inner(bands, own, paired, other, window):
    rows, cols, outs = own.shape
    span = cols + 2 * paired.shape[1]
    kernels = bands.shape[1] // BLOCK
    return kernel_call(
        functools.partial(backward_inner_kernel, window),
        [bands, own, paired, other],
        [
            pltpu.VMEM((kernels, (rows - 2) * cols, outs), jnp.bfloat16),
            pltpu.VMEM((rows, span, outs), jnp.bfloat16),
        ],
        [pltpu.VMEM((rows, span, outs), jnp.bfloat16)],
        12,
    )


def backward_edges_kernel(
    window, cols, bands, core, far, turned, filt, edge, extra
):
    rows, span, _ = turned.shape
    flip = mirror(span)
    even = even_band()
    for i, line in ((jnp.where(even, 1, 0), core), (jnp.where(even, 0, 1), far)):
        edge[i] = jnp.dot(flip, line[0:span], preferred_element_type=jnp.float32).astype(edge.dtype)
    none = jnp.zeros((core.shape[0] - span, 2 * LANES), jnp.float32)
    beside, across = core[span:, :].astype(jnp.float32), far[span:, :].astype(jnp.float32)
    above, below = jnp.where(even, across, beside), jnp.where(even, beside, across)
    spread_bands(packed_taps([none, none, above], window, bands.shape[2]), extra, 0)
    spread_bands(packed_taps([below, none, none], window, bands.shape[2]), extra, 1)
    last = rows - 1
    picks = (
        (extra[0], bands[0], bands[1], [turned.at[1], turned.at[0], edge.at[0]]),
        (bands[last - 1], bands[last], extra[1], [edge.at[1], turned.at[last], turned.at[last - 1]]),
    )
    for i, (above, here, below, lines) in enumerate(picks):
        band = adjoint_band(window, above, here, below)

        def write(first, k, value, base=i * cols):
            filt[k, base + first : base + first + BLOCK, :] = value

        adjoint_row(band, lines, cols, write)


def backward_edges(bands, core, far, turned, cols, window):
    _, span, outs = turned.shape
    kernels = bands.shape[1] // BLOCK
    return kernel_call(
        functools.partial(backward_edges_kernel, window, cols),
        [bands, core, far, turned],
        pltpu.VMEM((kernels, 2 * cols, outs), jnp.bfloat16),
        [
            pltpu.VMEM((2, span, outs), jnp.bfloat16),
            pltpu.VMEM((2,) + bands.shape[1:], jnp.bfloat16),
        ],
        8,
    )


def mixed_rows(source, mixing, first, count, cols, store):
    total = None
    for k in range(mixing.shape[0]):
        term = lax.dot_general(
            source[k, first * cols : (first + count) * cols, :],
            mixing[k],
            (((1,), (1,)), ((), ())),
            preferred_element_type=jnp.float32,
        )
        total = term if total is None else total + term
    total = total.astype(jnp.bfloat16)
    back = mirror(cols)
    for i in range(count):
        part = total[i * cols : (i + 1) * cols]
        store(i, jnp.dot(back, part, preferred_element_type=jnp.float32).astype(jnp.bfloat16))


def inner_mix_kernel(first, mixing, inner, out):
    def store(i, value):
        out[i] = value

    mixed_rows(inner, mixing, first, out.shape[0], out.shape[1], store)


def inner_mix(mixing, inner, first, count, cols):
    shape = (count, cols, mixing.shape[1])
    return kernel_call(
        functools.partial(inner_mix_kernel, first),
        [mixing, inner],
        pltpu.VMEM(shape, jnp.bfloat16),
        [],
        8,
    )


def back_mix_kernel(mixing, inner, filt, out, stage, sems):
    rows, cols, _ = out.shape
    copies = [
        pltpu.make_async_copy(inner, out.at[pl.ds(1, rows - 2)], sems.at[0]),
        pltpu.make_async_copy(stage.at[0], out.at[0], sems.at[1]),
        pltpu.make_async_copy(stage.at[1], out.at[rows - 1], sems.at[2]),
    ]
    copies[0].start()

    def store(i, value):
        stage[i] = value

    mixed_rows(filt, mixing, 0, 2, cols, store)
    copies[1].start()
    copies[2].start()
    for copy in copies:
        copy.wait()


def back_mix(mixing, inner, filt, rows):
    _, chans, _ = mixing.shape
    cols = filt.shape[1] // 2
    return kernel_call(
        back_mix_kernel,
        [mixing, inner, filt],
        jax.ShapeDtypeStruct((rows, cols, chans), jnp.bfloat16),
        [pltpu.VMEM((2, cols, chans), jnp.bfloat16), pltpu.SemaphoreType.DMA((3,))],
        8,
        far_out=True,
    )


def assemble_kernel(mine, other, out):
    half, _, piece, _ = mine.shape
    place = band_place(2 * half)
    for m in range(2 * half):
        source = mine[m] if m < half else other[m - half]
        start = pl.multiple_of((place ^ m) * piece, piece)
        out[:, pl.ds(start, piece), :] = source.astype(out.dtype)


def assemble(mine, other):
    half, share, piece, chans = mine.shape
    return kernel_call(
        assemble_kernel,
        [mine, other],
        jax.ShapeDtypeStruct((share, 2 * half * piece, chans), jnp.float32),
        [],
        4,
    )


def far_sum_kernel(skip, mine, other, out):
    out[...] = (mine[skip:] + other[...].astype(jnp.float32)).astype(out.dtype)


def far_sum(mine, other, skip):
    outs = pltpu.VMEM(other.shape, jnp.bfloat16)
    body = functools.partial(far_sum_kernel, skip)
    return kernel_call(body, [mine, other], outs, [], 4)


def reduced_gradient(keep, send):
    n_lat, n_lon = lax.axis_size("lat"), lax.axis_size("lon")
    high = lax.ppermute(send[1], "lat", swap("lat", 1))
    low = lax.ppermute(send[0], "lat", swap("lat", 1))
    send = (keep[1] + high.astype(jnp.float32)).astype(jnp.bfloat16)
    keep = keep[0] + low.astype(jnp.float32)
    cut = n_lon // 2
    totals = []
    for part in (slice(cut, n_lon), slice(0, cut)):
        mine, sent, mask = keep[:, part], send[:, part], 2
        while True:
            other = lax.ppermute(sent, "lat", swap("lat", mask))
            mask *= 2
            if mask >= n_lat and not totals:
                source, skip = (keep, cut) if mask == 4 else (mine, 0)
                wire = far_sum(source[0], other[0], skip)
                totals.append(None)
                break
            total = mine + other.astype(jnp.float32)
            if mask >= n_lat:
                totals.append(total[0])
                break
            half = total.shape[0] // 2
            mine, sent = total[:half], total[half:].astype(jnp.bfloat16)
    near_part = totals[1]
    piece = near_part[0]
    wires = [near_part.astype(jnp.bfloat16), wire]
    for s in range(1, n_lon):
        other = lax.ppermute(wires[s // cut][s % cut], "lon", swap("lon", s))
        piece = piece + other.astype(jnp.float32)
    pieces = piece.astype(jnp.bfloat16)[None]
    while mask > 1:
        mask //= 2
        other = lax.ppermute(pieces, "lat", swap("lat", mask))
        if mask > 1:
            pieces = jnp.concatenate([pieces, other], axis=0)
    return assemble(pieces, other)


def on_device(field_in, quadrature, half_width, mixing, cotangent):
    rows, cols, chans = field_in.shape
    kernels, _, outs = mixing.shape
    taps = quadrature.shape[-1]
    rim = (taps - 1) // 2
    n_lat, n_lon = lax.axis_size("lat"), lax.axis_size("lon")
    groups = split_rows(rows)
    outer = groups[0]

    def beside(pair):
        count = lax.axis_size("lon")
        other = [(i, (i + 1) % count) for i in range(1, count, 2)]
        return [
            lax.ppermute(pair[0], "lon", swap("lon", 1)),
            lax.ppermute(pair[1], "lon", other + [(j, i) for i, j in other]),
        ]

    def bands_beside(pair):
        across = [(i, i + 1) for i in range(1, lax.axis_size("lat") - 1, 2)]
        far = lax.ppermute(pair[1], "lat", across + [(j, i) for i, j in across])
        core = lax.ppermute(pair[0], "lat", swap("lat", 1))
        return core, far

    window = taps - 1 + BLOCK
    sides = rims(field_in, rim, groups)
    outer_sides = beside(sides[0:2])
    inner_sides = beside(sides[2:4])
    *sides, field_near, cot_near, taps_near, reach = loads(
        field_in, cotangent, quadrature, half_width, rim
    )
    g_sides = beside(sides)
    bands, basis_edges = band_matrices(reach, taps_near)
    picks = (0, len(outer) - 1)
    sent = edge_rows(field_near, *outer_sides, picks, [])
    f_core, f_far = bands_beside(sent)

    flat_cot = cot_near.reshape(rows * cols, outs)
    filtered, *send = forward(
        bands,
        field_near,
        f_core,
        f_far,
        flat_cot,
        groups,
        outer_sides + inner_sides,
        kernels,
        n_lat,
        n_lon,
    )
    keep = kept(filtered, flat_cot, kernels, n_lat, n_lon)
    weight_grad = reduced_gradient(keep, send)
    field_out = kernel_call(
        mix_kernel,
        [filtered, mixing.reshape(kernels * chans, outs)],
        jax.ShapeDtypeStruct((rows * cols, outs), jnp.bfloat16),
        [],
        8,
    )
    sent = edge_rows(cot_near, *g_sides, (0, rows - 1), [basis_edges])
    g_core, g_far = bands_beside(sent)
    inner, turned = backward_inner(bands, cot_near, *g_sides, window)
    edge = backward_edges(bands, g_core, g_far, turned, cols, window)
    inner = inner_mix(mixing, inner, 0, rows - 2, cols)
    input_grad = back_mix(mixing, inner, edge, rows)
    return (
        field_out.reshape(rows, cols, outs),
        input_grad,
        weight_grad,
    )


def solution(mesh):
    return jax.shard_map(
        on_device,
        mesh=mesh,
        in_specs=(
            P(("ens", "lat"), "lon", None),
            P("lat", None, None, None),
            P("lat"),
            P(),
            P(("ens", "lat"), "lon", None),
        ),
        out_specs=(
            P(("ens", "lat"), "lon", None),
            P(("ens", "lat"), "lon", None),
            P("lon", "ens", None),
        ),
        check_vma=False,
    )
```
